256 devices in a mesh: ep: 64 (over z, x, core), tp: 4 (over y).
Axes of the slice: x: 4, y: 4, z: 8, core: 2. Of those that a mesh axis runs over, the one named last changes fastest.
Arguments:
- tokens: bfloat16 [8192, 2048], P('ep', 'tp'), may hold values from -6 to 6
- cotangent: bfloat16 [8192, 2048], P('ep', 'tp'), may hold values from -12 to 12
- route_weights: bfloat16 [8192, 8], P('ep'), may hold values from 0.049804688 to 0.59765625
- routes: int32 [8192, 8], P('ep'), may hold values from 0 to 63, all different within a row; in each aligned block of 128 rows (0 to 127, 128 to 255, ...) at most 24 rows name the same one
- grid_gate: bfloat16 [64, 768, 2048], P('ep', 'tp'), may hold values from -4 to 4
- latent_gate: bfloat16 [64, 768, 2048], P('ep', 'tp'), may hold values from -0.5 to 0.5
- scale_gate: float32 [64, 768], P('ep', 'tp'), may hold values from 0.006 to 0.02
- grid_up: bfloat16 [64, 768, 2048], P('ep', 'tp'), may hold values from -4 to 4
- latent_up: bfloat16 [64, 768, 2048], P('ep', 'tp'), may hold values from -0.5 to 0.5
- scale_up: float32 [64, 768], P('ep', 'tp'), may hold values from 0.006 to 0.02
- grid_down: bfloat16 [64, 768, 2048], P('ep', 'tp'), may hold values from -4 to 4
- latent_down: bfloat16 [64, 768, 2048], P('ep', 'tp'), may hold values from -0.5 to 0.5
- scale_down: float32 [64, 2048], P('ep'), may hold values from 0.006 to 0.02
Outputs:
- grad_latent_gate: float32 [64, 768, 2048], P('ep', 'tp')
- grad_latent_up: float32 [64, 768, 2048], P('ep', 'tp')
- grad_latent_down: float32 [64, 768, 2048], P('ep', 'tp')
- token_grad: bfloat16 [8192, 2048], P('ep', 'tp')
- route_grad: float32 [8192, 8], P('ep')
The draws below stay inside these ranges and needn't reach their ends.
Inputs may be any that keep to these rules, and one draw needn't show every extreme that they name: `routes`: each row names 8 different experts. In each aligned block of 128 tokens (the tokens of one index of ep), no expert is named by more than 24 of them, a bound that some block reaches.
All inputs are finite; a program needn't handle non-finite values.
Results may differ from the reference program's by a relative error of at most 0.006.
Values may be sent and summed in bfloat16 or wider, within the bound.
A program may use at most 192 MiB of HBM per device.

```python
import math
import jax
import jax.numpy as jnp
import numpy as np
from jax import lax

D = 2048
FF = 768
TOP = 8
TOK_DEV = 128
EXPERTS = 64
CAP = 24
TOKENS = 8192


def block_levels(key, dims, cuts, least, top_value):
    def one(dim, shards_of):
        steps = jax.random.uniform(jax.random.fold_in(jax.random.fold_in(key, 6), dim), (shards_of,), jnp.float32, least / len(cuts), top_value / len(cuts))
        return jnp.repeat(jnp.exp(steps), dims[dim] // shards_of).reshape((-1,) + (1,) * (len(dims) - dim - 1))

    gain = one(*cuts[0])
    for cut in cuts[1:]:
        gain = gain * one(*cut)
    return gain


def deal_out(own_key, own, number, rows, count, top, bound, lean):
    order = jax.random.permutation(own_key, count)
    heavy_load, usual = portions_of(count, rows * top, bound, lean, True), portions_of(count, rows * top, bound, lean, False)
    places = jnp.arange(count)

    def named(lengths, turn):
        used = int((lengths > 0).sum())
        fixed = max(1, used // 4)
        passed = fixed + (places - fixed + turn * (used - fixed)) % max(1, count - fixed)
        return jnp.zeros((count,), jnp.int32).at[order[jnp.where(places < fixed, places, passed)]].set(jnp.asarray(lengths, jnp.int32))

    lengths = jnp.where(number % 4 == 0, named(heavy_load, number // 4), named(usual, number - number // 4 - 1))
    mixed = jax.random.permutation(jax.random.fold_in(own, 3), count)
    donor, sink = mixed[0:count // 2 * 2:2], mixed[1:count // 2 * 2:2]
    room = jnp.minimum(lengths[donor] - 1, bound - lengths[sink]) // 2
    room = jnp.where((donor == order[0]) | (sink == order[0]) | (lengths[sink] == 0), 0, jnp.maximum(room, 0))
    passed = jax.random.randint(jax.random.fold_in(own, 4), (count // 2,), 0, 1 << 20) % (room + 1)
    lengths = lengths.at[donor].add(-passed).at[sink].add(passed)
    items = jnp.searchsorted(jnp.cumsum(lengths), jnp.arange(rows * top), side="right").astype(jnp.int32)
    listing = items.reshape(top, rows).T
    listing = listing[jax.random.permutation(jax.random.fold_in(own, 1), rows)]
    turn = jax.random.randint(jax.random.fold_in(own, 2), (rows, 1), 0, top)
    return jnp.take_along_axis(listing, (jnp.arange(top)[None, :] + turn) % top, axis=1)


def portions_of(amount, total, bound, skew, full):
    loads = [(1 << 20) // math.isqrt(grade ** skew) + 1 for grade in range(1, amount + 1)]
    largest = bound if full else min(bound, max(-(-total // amount), total * loads[0] // sum(loads)))
    least = 1 if total - largest >= amount - 1 else 0
    counts, surplus = [largest] + [least] * (amount - 1), total - largest - least * (amount - 1)
    while surplus > 0:
        candidates = [i for i in range(1, amount) if counts[i] < largest] or [i for i in range(1, amount) if counts[i] < bound]
        mass, left = sum([loads[i] for i in candidates]), surplus
        for i in candidates:
            addition = min(bound - counts[i], max(1, left * loads[i] // mass), surplus)
            counts[i] = counts[i] + addition
            surplus = surplus - addition
    return np.array(counts)


def gaussian(own_key, extent, scale, limit, split=(), kind=jnp.bfloat16):
    level = block_levels(own_key, extent, split, -0.22, 0.18) if split else 1.0
    values = jax.random.normal(own_key, extent, jnp.float32) * scale * level
    return jnp.minimum(jnp.maximum(values, -limit), limit).astype(kind)


def setup_inputs(seed: int = 0) -> dict:
    arg_keys = jax.random.split(jax.random.key(seed), 14)
    tokens = gaussian(arg_keys[0], (TOKENS, D), 1.0, 6.0, ((0, 64), (1, 4)))
    cotangent = gaussian(arg_keys[1], (TOKENS, D), 2.0, 12.0, ((0, 64), (1, 4)))
    route_weights = jnp.clip(0.049804688 + 0.54785156 * jax.random.uniform(arg_keys[2], (TOKENS, TOP), jnp.float32) ** block_levels(arg_keys[2], (TOKENS, TOP), ((0, 64),), -0.2, 0.2), 0.049804688, 0.59765625).astype(jnp.bfloat16)
    routes_keys = jax.random.split(jax.random.fold_in(arg_keys[3], 1), TOKENS // TOK_DEV)
    routes_turns = jax.random.permutation(jax.random.fold_in(arg_keys[3], 3), TOKENS // TOK_DEV)
    routes = jax.vmap(lambda own, number: deal_out(jax.random.fold_in(arg_keys[3], 2), own, number, TOK_DEV, EXPERTS, TOP, CAP, 2))(routes_keys, routes_turns).reshape((TOKENS, TOP))
    grid_gate = gaussian(arg_keys[4], (EXPERTS, FF, D), 1.0, 4.0, ((0, 64), (1, 4)))
    latent_gate = jnp.clip(jax.random.uniform(arg_keys[5], (EXPERTS, FF, D), jnp.float32, -0.5, 0.5) * block_levels(arg_keys[5], (EXPERTS, FF, D), ((0, 64), (1, 4)), -0.4, 0.0), -0.5, 0.5).astype(jnp.bfloat16)
    scale_gate = jnp.clip(jnp.exp(math.log(0.02) - 1.2039728 * jax.random.uniform(arg_keys[6], (EXPERTS, FF), jnp.float32) ** block_levels(arg_keys[6], (EXPERTS, FF), ((0, 64), (1, 4)), -0.2, 0.2)), 0.006, 0.02)
    grid_up = gaussian(arg_keys[7], (EXPERTS, FF, D), 1.0, 4.0, ((0, 64), (1, 4)))
    latent_up = jnp.clip(jax.random.uniform(arg_keys[8], (EXPERTS, FF, D), jnp.float32, -0.5, 0.5) * block_levels(arg_keys[8], (EXPERTS, FF, D), ((0, 64), (1, 4)), -0.4, 0.0), -0.5, 0.5).astype(jnp.bfloat16)
    scale_up = jnp.clip(jnp.exp(math.log(0.02) - 1.2039728 * jax.random.uniform(arg_keys[9], (EXPERTS, FF), jnp.float32) ** block_levels(arg_keys[9], (EXPERTS, FF), ((0, 64), (1, 4)), -0.2, 0.2)), 0.006, 0.02)
    grid_down = gaussian(arg_keys[10], (EXPERTS, FF, D), 1.0, 4.0, ((0, 64), (1, 4)))
    latent_down = jnp.clip(jax.random.uniform(arg_keys[11], (EXPERTS, FF, D), jnp.float32, -0.5, 0.5) * block_levels(arg_keys[11], (EXPERTS, FF, D), ((0, 64), (1, 4)), -0.4, 0.0), -0.5, 0.5).astype(jnp.bfloat16)
    scale_down = jnp.clip(jnp.exp(math.log(0.02) - 1.2039728 * jax.random.uniform(arg_keys[12], (EXPERTS, D), jnp.float32) ** block_levels(arg_keys[12], (EXPERTS, D), ((0, 64),), -0.2, 0.2)), 0.006, 0.02)
    return {"tokens": tokens, "cotangent": cotangent, "route_weights": route_weights, "routes": routes, "grid_gate": grid_gate, "latent_gate": latent_gate, "scale_gate": scale_gate, "grid_up": grid_up, "latent_up": latent_up, "scale_up": scale_up, "grid_down": grid_down, "latent_down": latent_down, "scale_down": scale_down}


temper = 0.25
grad_factor = 8.0


def soften_rows(grid, latent, scale):
    level = grid.astype(jnp.float32) + 0.5 * (1.0 + jnp.tanh(latent.astype(jnp.float32) / temper))
    return level * scale[:, None]


def soften_cols(grid, latent, scale):
    level = grid.astype(jnp.float32) + 0.5 * (1.0 + jnp.tanh(latent.astype(jnp.float32) / temper))
    return level * scale[None, :]


def latent_rows(grad_weight, latent, scale):
    slope = jnp.tanh(latent.astype(jnp.float32) / temper)
    return grad_factor * grad_weight * scale[:, None] * (1.0 - slope * slope) / (2.0 * temper)


def latent_cols(grad_weight, latent, scale):
    slope = jnp.tanh(latent.astype(jnp.float32) / temper)
    return grad_factor * grad_weight * scale[None, :] * (1.0 - slope * slope) / (2.0 * temper)


def block_slots(block_routes, experts, capacity):
    flat = block_routes.reshape(-1).astype(jnp.int32)
    columns = jnp.arange(experts, dtype=jnp.int32)
    onehot = (flat[:, None] == columns[None, :]).astype(jnp.int32)
    earlier = jnp.cumsum(onehot, axis=0) - onehot
    return flat * capacity + jnp.sum(earlier * onehot, axis=1).astype(jnp.int32)


def entry_table(dest, entries, experts, capacity):
    table = jnp.full((experts * capacity,), entries, jnp.int32)
    return table.at[dest].set(jnp.arange(entries, dtype=jnp.int32))


def expert_backward(rows_x, rows_y, rows_p, w_gate, w_up, w_down):
    rowwise = (((1,), (1,)), ((), ()))
    gate = lax.dot_general(rows_x, w_gate, rowwise, preferred_element_type=jnp.float32)
    upper = lax.dot_general(rows_x, w_up, rowwise, preferred_element_type=jnp.float32)
    sigma = jax.nn.sigmoid(gate)
    active = gate * sigma
    hidden = active * upper
    weight = rows_p.astype(jnp.float32)[:, None]
    scaled = (hidden * weight).astype(jnp.bfloat16)
    back_hidden = lax.dot_general(rows_y, w_down, rowwise, preferred_element_type=jnp.float32)
    score = jnp.sum(hidden * back_hidden, axis=1)
    delta = back_hidden * weight
    grad_gate = (delta * upper * sigma * (1.0 + gate * (1.0 - sigma))).astype(jnp.bfloat16)
    grad_upper = (delta * active).astype(jnp.bfloat16)
    contract = (((0,), (0,)), ((), ()))
    grad_wg = lax.dot_general(grad_gate, rows_x, contract, preferred_element_type=jnp.float32)
    grad_wu = lax.dot_general(grad_upper, rows_x, contract, preferred_element_type=jnp.float32)
    grad_wd = lax.dot_general(scaled, rows_y, contract, preferred_element_type=jnp.float32)
    back_rows = jnp.dot(grad_gate, w_gate, preferred_element_type=jnp.float32)
    back_rows = back_rows + jnp.dot(grad_upper, w_up, preferred_element_type=jnp.float32)
    return grad_wg, grad_wu, grad_wd, back_rows, score


def reference(tokens, cotangent, route_weights, routes, grid_gate, latent_gate, scale_gate, grid_up, latent_up, scale_up, grid_down, latent_down, scale_down):
    blocks = TOKENS // TOK_DEV
    entries = TOK_DEV * TOP
    dest = jax.vmap(lambda r: block_slots(r, EXPERTS, CAP))(routes.reshape(blocks, TOK_DEV, TOP))
    local = jax.vmap(lambda d: entry_table(d, entries, EXPERTS, CAP))(dest)
    offsets = (jnp.arange(blocks, dtype=jnp.int32) * entries)[:, None]
    global_entry = jnp.where(local == entries, TOKENS * TOP, local + offsets).astype(jnp.int32)
    table = global_entry.reshape(blocks, EXPERTS, CAP).transpose(1, 0, 2).reshape(EXPERTS, blocks * CAP)
    tokens_pad = jnp.concatenate([tokens, jnp.zeros((1, D), jnp.bfloat16)], axis=0)
    cotan_pad = jnp.concatenate([cotangent, jnp.zeros((1, D), jnp.bfloat16)], axis=0)
    weights_pad = jnp.concatenate([route_weights.reshape(-1), jnp.zeros((1,), jnp.bfloat16)], axis=0)

    def step(carry, inputs):
        token_acc, score_acc = carry
        entry, g_grid, g_lat, g_scale, u_grid, u_lat, u_scale, d_grid, d_lat, d_scale = inputs
        token = (entry // TOP).astype(jnp.int32)
        rows_x = tokens_pad[token]
        rows_y = cotan_pad[token]
        rows_p = weights_pad[entry]
        w_gate = soften_rows(g_grid, g_lat, g_scale).astype(jnp.bfloat16)
        w_up = soften_rows(u_grid, u_lat, u_scale).astype(jnp.bfloat16)
        w_down = soften_cols(d_grid, d_lat, d_scale).astype(jnp.bfloat16)
        grad_wg, grad_wu, grad_wd, back_rows, score = expert_backward(rows_x, rows_y, rows_p, w_gate, w_up, w_down)
        token_acc = token_acc.at[token].add(back_rows)
        score_acc = score_acc.at[entry].add(score)
        outs = (latent_rows(grad_wg, g_lat, g_scale), latent_rows(grad_wu, u_lat, u_scale), latent_cols(grad_wd, d_lat, d_scale))
        return (token_acc, score_acc), outs

    start = (jnp.zeros((TOKENS + 1, D), jnp.float32), jnp.zeros((TOKENS * TOP + 1,), jnp.float32))
    inputs = (table, grid_gate, latent_gate, scale_gate, grid_up, latent_up, scale_up, grid_down, latent_down, scale_down)
    (token_acc, score_acc), (grad_gate, grad_upper, grad_lower) = lax.scan(step, start, inputs)
    token_grad = token_acc[:TOKENS].astype(jnp.bfloat16)
    route_grad = score_acc[:TOKENS * TOP].reshape(TOKENS, TOP)
    return grad_gate, grad_upper, grad_lower, token_grad, route_grad
```

```python
import jax
import jax.numpy as jnp
from jax import lax
from jax.experimental import pallas as pl
from jax.experimental.pallas import tpu as pltpu
from jax.sharding import PartitionSpec as P

temper = 0.25
grad_factor = 8.0

NZ, NX, NY = 8, 4, 4
D, FF, TOK, EXPERTS, CAP = 2048, 768, 128, 64, 24
QD = D // NY
HID = FF // NY
HALF = HID // 2
PAIR = 2 * CAP
ROWS = NX * 2 * PAIR
WIDE = 2 * D + 128
BACK = D + 128
F32, BF16 = jnp.float32, jnp.bfloat16
MESH = pl.DeviceIdType.MESH


def dot_nt(a, b):
    return lax.dot_general(a, b, (((1,), (1,)), ((), ())), preferred_element_type=F32)


def dot_tn(a, b):
    return lax.dot_general(a, b, (((0,), (0,)), ((), ())), preferred_element_type=F32)


def dot_nn(a, b):
    return lax.dot_general(a, b, (((1,), (0,)), ((), ())), preferred_element_type=F32)


def kernel(
    tok_ref, cot_ref, rt_ref, wt_ref, routes_ref, wg_ref, wu_ref, wd_ref,
    sums_ref, tgrad_ref, rgrad_ref,
    wf, grad, rr, blk, aux, sendbuf, rows, smat, gs, us, ap, dg, du, br, rb, part, zb, zt, fb, stage, tg, sc, fin,
    ws, wr, wl, gsend, grecv, ys, yr, zs, zr, xs, xr, bs, brecv, zbs, zbr, ls, lr,
):
    i, y = lax.axis_index("ep"), lax.axis_index("tp")
    z, x, c = i // 8, lax.rem(i, 8) // 2, lax.rem(i, 2)
    own = 2 * x + c
    column = c == y // 2
    odd = lax.rem(z + y, 2) == 1
    yb = 2 * c + lax.rem(z, 2)
    owner = y == yb

    def up(n):
        return lax.rem(y + n + NY, NY)

    def zat(n):
        return lax.rem(z + n + NZ, NZ)

    def zdev(n):
        return (8 * zat(n) + own, y)

    def remote(src, dst, send, recv, dev):
        return pltpu.make_async_remote_copy(
            src_ref=src, dst_ref=dst, send_sem=send, recv_sem=recv, device_id=dev, device_id_type=MESH
        )

    def arrived(dst, recv, send):
        remote(dst, dst, send, recv, (i, up(1))).wait_recv()

    def sent(src, send, recv):
        remote(src, src, send, recv, (i, up(1))).wait_send()

    def mult(v, n):
        return pl.multiple_of(v, n)

    barrier = pltpu.get_barrier_semaphore()
    for d in range(1, NY):
        pl.semaphore_signal(barrier, inc=1, device_id=(i, up(d)), device_id_type=MESH)
    for d in (1, -1):
        pl.semaphore_signal(barrier, inc=1, device_id=zdev(d), device_id_type=MESH)
    for d in range(1, 8):
        pl.semaphore_signal(barrier, inc=1, device_id=(8 * z + lax.rem(own + d, 8), y), device_id_type=MESH)

    weights = (wg_ref, wu_ref, wd_ref)
    stage[:, 0:QD] = tok_ref[...]
    stage[:, QD:] = cot_ref[...]

    def block(s, f):
        return blk.at[s // 2, f, pl.ds(mult(TOK * lax.rem(s, 2), TOK), TOK), :]

    s_own = z // 2

    @pl.when(owner)
    def _():
        expert = lax.broadcasted_iota(jnp.int32, (EXPERTS, TOK), 0)
        hit = jnp.zeros((EXPERTS, TOK), F32)
        weight = jnp.zeros((EXPERTS, TOK), F32)
        for k in range(8):
            same = expert == rt_ref[k : k + 1, :]
            hit = hit + jnp.where(same, 1.0, 0.0)
            weight = weight + jnp.where(same, wt_ref[k : k + 1, :], 0.0)
        before = lax.broadcasted_iota(jnp.int32, (TOK, TOK), 0) < lax.broadcasted_iota(jnp.int32, (TOK, TOK), 1)
        slot = dot_nn(hit.astype(BF16), jnp.where(before, 1.0, 0.0).astype(BF16))
        aux[s_own, 0:EXPERTS, :] = jnp.where(hit > 0.0, slot, -100.0)
        aux[s_own, EXPERTS:, :] = weight

    pl.semaphore_wait(barrier, 3 + 2 + 7)

    @pl.when(jnp.logical_not(owner))
    def _():
        remote(stage, block(s_own, y), ys, yr.at[y], (i, yb)).start()

    def wpart(m, n, h):
        return wf.at[m, pl.ds(mult(HID * up(n) + HALF * h, HALF), HALF), :]

    for m in range(3):
        for h in range(2):
            src = weights[m].at[pl.ds(HALF * h, HALF), :]
            remote(src, wpart(m, 0, h), ws.at[m, 0, h], wr.at[m, 0, h], (i, up(1))).start()
            back = weights[m].at[pl.ds(HALF * (1 - h), HALF), :]
            remote(back, wpart(m, 0, 1 - h), ws.at[m, 1, 1 - h], wr.at[m, 1, 1 - h], (i, up(-1))).start()
        pltpu.make_async_copy(
            weights[m], wf.at[m, pl.ds(mult(HID * y, HALF), HID), :], wl.at[m]
        ).start()

    def piece(s, f):
        return aux.at[s] if f == 4 else block(s, f)

    def zcopy(n, s, f, k):
        return remote(piece(s, f), piece(s, f), zs.at[(1 - n) // 2, k, f], zr.at[s, f], zdev(n))

    @pl.when(jnp.logical_and(column, jnp.logical_not(odd)))
    def _():
        block(s_own, y)[...] = stage[...]
        for d in range(1, NY):
            arrived(block(s_own, up(d)), yr.at[up(d)], ys)
        for f in (4, 0, 1, 2, 3):
            zcopy(1, s_own, f, 0).start()
            zcopy(-1, s_own, f, 0).start()
        s_a, s_b, s_c = zat(-2) // 2, zat(2) // 2, zat(4) // 2
        for f in (4, 0, 1, 2, 3):
            zcopy(1, s_a, f, 1).wait_recv()
            zcopy(1, s_a, f, 1).start()
            zcopy(-1, s_b, f, 1).wait_recv()
            zcopy(-1, s_b, f, 1).start()
        for f in (4, 0, 1, 2, 3):
            zcopy(1, s_c, f, 1).wait_recv()

    @pl.when(jnp.logical_and(column, odd))
    def _():
        s_a, s_b, s_c, s_d = zat(-1) // 2, zat(1) // 2, zat(-3) // 2, zat(3) // 2
        for f in (4, 0, 1, 2, 3):
            zcopy(1, s_a, f, 0).wait_recv()
            zcopy(1, s_a, f, 0).start()
            zcopy(-1, s_b, f, 0).wait_recv()
            zcopy(-1, s_b, f, 0).start()
        for f in (4, 0, 1, 2, 3):
            zcopy(1, s_c, f, 1).wait_recv()
            if f in (4, 0, 1):
                zcopy(1, s_c, f, 1).start()
            zcopy(1, s_d, f, 1).wait_recv()
            if f in (2, 3):
                zcopy(-1, s_d, f, 1).start()

    def rowpart(xsrc, pair):
        return rows.at[pl.ds(mult(2 * PAIR * xsrc + PAIR * pair, PAIR), PAIR), :]

    @pl.when(column)
    def _():
        for pair in range(2):
            slots = [aux[2 * pair + b, pl.ds(mult(8 * z, 8), 8), :] + float(CAP * b) for b in range(2)]
            gains = [aux[2 * pair + b, pl.ds(mult(EXPERTS + 8 * z, 8), 8), :] for b in range(2)]
            slots = jnp.concatenate(slots, axis=1)
            gains = jnp.concatenate(gains, axis=1)
            place = lax.broadcasted_iota(jnp.int32, (PAIR, 2 * TOK), 0).astype(F32)
            for j in range(8):
                chosen = place == slots[j : j + 1, :]
                smat[pair, PAIR * j : PAIR * (j + 1), :] = jnp.where(chosen, 1.0, 0.0).astype(BF16)
                gain = jnp.sum(jnp.where(chosen, gains[j : j + 1, :], 0.0), axis=1, keepdims=True)
                sendbuf[pair, PAIR * j : PAIR * (j + 1), 2 * D :] = jnp.broadcast_to(gain, (PAIR, 128)).astype(BF16)
            for f in range(NY):
                picked = dot_nn(smat[pair], blk[pair, f]).astype(BF16)
                sendbuf[pair, :, QD * f : QD * (f + 1)] = picked[:, 0:QD]
                sendbuf[pair, :, D + QD * f : D + QD * (f + 1)] = picked[:, QD:]
            for d in range(8):
                j = lax.rem(own + d, 8)
                src = sendbuf.at[pair, pl.ds(mult(PAIR * j, PAIR), PAIR), :]
                if d == 0:
                    pltpu.make_async_copy(src, rowpart(x, pair), xr.at[pair, x]).start()
                else:
                    remote(src, rowpart(x, pair), xs.at[pair, d], xr.at[pair, x], (8 * z + j, y)).start()

    for m in range(3):
        arrived(wpart(m, -1, 0), wr.at[m, 0, 0], ws.at[m, 0, 0])
        remote(wpart(m, -1, 0), wpart(m, -1, 0), ws.at[m, 0, 2], wr.at[m, 0, 2], (i, up(1))).start()
        arrived(wpart(m, 1, 1), wr.at[m, 1, 1], ws.at[m, 0, 0])
        remote(wpart(m, 1, 1), wpart(m, 1, 1), ws.at[m, 1, 2], wr.at[m, 1, 2], (i, up(-1))).start()

    def weight_whole(m):
        arrived(wpart(m, -1, 1), wr.at[m, 0, 1], ws.at[m, 0, 0])
        arrived(wpart(m, 1, 0), wr.at[m, 1, 0], ws.at[m, 0, 0])
        arrived(wpart(m, 2, 0), wr.at[m, 0, 2], ws.at[m, 0, 0])
        arrived(wpart(m, 2, 1), wr.at[m, 1, 2], ws.at[m, 0, 0])
        pltpu.make_async_copy(
            weights[m], wf.at[m, pl.ds(mult(HID * y, HALF), HID), :], wl.at[m]
        ).wait()

    for xsrc in range(NX):
        for pair in range(2):
            arrived(rowpart(xsrc, pair), xr.at[pair, xsrc], ys)

    weight = rows[:, 2 * D : 2 * D + 1].astype(F32)

    def gpart(m, n, h):
        return grad.at[m, pl.ds(mult(HID * up(n) + HALF * h, HALF), HALF), :]

    def grad_first(m):
        remote(gpart(m, 2, 0), rr.at[m, 0], gsend.at[m, 0], grecv.at[m, 0], (i, up(1))).start()
        remote(gpart(m, 2, 1), rr.at[m, 1], gsend.at[m, 1], grecv.at[m, 1], (i, up(-1))).start()
        remote(gpart(m, 1, 1), rr.at[m, 3], gsend.at[m, 3], grecv.at[m, 3], (i, up(1))).start()
        remote(gpart(m, -1, 0), rr.at[m, 5], gsend.at[m, 5], grecv.at[m, 5], (i, up(-1))).start()

    def grad_pass(m):
        for k, n, h, to in ((0, 1, 0, 1), (1, -1, 1, -1)):
            arrived(rr.at[m, k], grecv.at[m, k], ys)
            mine = gpart(m, n, h)
            mine[...] = (mine[...].astype(F32) + rr[m, k].astype(F32)).astype(BF16)
            remote(mine, rr.at[m, 2 + 2 * k], gsend.at[m, 2 + 2 * k], grecv.at[m, 2 + 2 * k], (i, up(to))).start()

    tiles = FF // 256

    def hidden(t):
        return pl.ds(mult(256 * t, 256), 256)

    def outer(m, left, at, t):
        turned = left.astype(F32).T.astype(BF16)
        for h in range(2):
            cols = slice(1024 * h, 1024 * (h + 1))
            grad[m, hidden(t), cols] = dot_nn(turned, rows[:, at + 1024 * h : at + 1024 * (h + 1)]).astype(BF16)

    weight_whole(0)
    weight_whole(1)

    @pl.loop(0, tiles)
    def _(t):
        g = dot_nt(rows[:, 0:D], wf[0, hidden(t), :])
        u = dot_nt(rows[:, 0:D], wf[1, hidden(t), :])
        gs[t] = g
        us[t] = u
        outer(2, (g * jax.nn.sigmoid(g) * u * weight).astype(BF16), D, t)

    grad_first(2)
    weight_whole(2)
    ap[...] = jnp.zeros_like(ap)

    @pl.loop(0, tiles)
    def _(t):
        g, u = gs[t], us[t]
        bh = dot_nt(rows[:, D : 2 * D], wf[2, hidden(t), :])
        sigma = jax.nn.sigmoid(g)
        active = g * sigma
        ap[...] += jnp.sum(active * u * bh, axis=1, keepdims=True)
        delta = bh * weight
        dg[t] = (delta * u * sigma * (1.0 + g * (1.0 - sigma))).astype(BF16)
        du[t] = (delta * active).astype(BF16)

    for h in range(2):
        cols = slice(1024 * h, 1024 * (h + 1))
        total = None
        for t in range(tiles):
            term = dot_nn(dg[t], wf[0, 256 * t : 256 * (t + 1), cols])
            term = term + dot_nn(du[t], wf[1, 256 * t : 256 * (t + 1), cols])
            total = term if total is None else total + term
        br[:, cols] = total.astype(BF16)
    score = ap[...]
    high = score.astype(BF16).astype(F32)
    low = score - high
    lane = lax.broadcasted_iota(jnp.int32, (ROWS, 128), 1)
    br[:, D:] = (jnp.where(lane == i, high, 0.0) + jnp.where(lane == i + EXPERTS, low, 0.0)).astype(BF16)

    def backpart(xsrc, pair):
        return br.at[pl.ds(mult(2 * PAIR * xsrc + PAIR * pair, PAIR), PAIR), :]

    def backslot(j, pair):
        return rb.at[pair, pl.ds(mult(PAIR * j, PAIR), PAIR), :]

    def back_send(d, pair):
        xsrc = lax.rem(x + d, NX)
        return remote(
            backpart(xsrc, pair), backslot(own, pair), bs.at[pair, d], brecv.at[pair, own],
            (8 * z + 2 * xsrc + y // 2, y),
        )

    def back_local(pair):
        return pltpu.make_async_copy(backpart(x, pair), backslot(own, pair), brecv.at[pair, own])

    for pair in range(2):
        for d in range(1, NX):
            back_send(d, pair).start()

        @pl.when(column)
        def _():
            back_local(pair).start()

        @pl.when(jnp.logical_not(column))
        def _():
            back_send(0, pair).start()

    @pl.loop(0, tiles)
    def _(t):
        outer(0, dg[t], 0, t)

    grad_first(0)

    @pl.loop(0, tiles)
    def _(t):
        outer(1, du[t], 0, t)

    grad_first(1)
    grad_pass(2)

    def plane(s):
        return part[s // 2, pl.ds(mult(TOK * lax.rem(s, 2), TOK), TOK), :]

    def zback(k, n, lanes=slice(None)):
        slot = k
        return remote(zt.at[k, :, lanes], zb.at[slot, :, lanes], zbs.at[k], zbr.at[slot], zdev(n))

    left, right = slice(0, 1024), slice(1024, BACK)

    @pl.when(column)
    def _():
        for pair in range(2):
            for j in range(8):
                arrived(backslot(j, pair), brecv.at[pair, j], ys)
            for cols in (slice(0, 1024), slice(1024, BACK)):
                part[pair, :, cols] = dot_tn(smat[pair], rb[pair, :, cols])

    @pl.when(jnp.logical_and(column, jnp.logical_not(odd)))
    def _():
        s_a, s_b, s_c = zat(-2) // 2, zat(2) // 2, zat(4) // 2
        far = plane(s_c).astype(BF16)
        zt[0] = far
        zt[1] = far
        zback(0, -1, left).start()
        zback(1, 1, right).start()
        zback(0, -1).wait_recv()
        zt[2] = (plane(s_a) + zb[0].astype(F32)).astype(BF16)
        zback(2, -1).start()
        zback(1, 1).wait_recv()
        zt[3] = (plane(s_b) + zb[1].astype(F32)).astype(BF16)
        zback(3, 1).start()
        zback(2, -1).wait_recv()
        zback(3, 1).wait_recv()
        fb[...] = (plane(s_own) + zb[2].astype(F32) + zb[3].astype(F32)).astype(BF16)
        zback(0, -1, left).wait_send()
        zback(1, 1, right).wait_send()
        zback(2, -1).wait_send()
        zback(3, 1).wait_send()

    @pl.when(jnp.logical_and(column, odd))
    def _():
        s_a, s_b, s_c, s_d = zat(-1) // 2, zat(1) // 2, zat(-3) // 2, zat(3) // 2
        zback(0, -1, left).wait_recv()
        zt[0, :, left] = (plane(s_c)[:, left] + zb[0, :, left].astype(F32)).astype(BF16)
        zt[0, :, right] = plane(s_c)[:, right].astype(BF16)
        zback(0, -1).start()
        zback(1, 1, right).wait_recv()
        zt[1, :, left] = plane(s_d)[:, left].astype(BF16)
        zt[1, :, right] = (plane(s_d)[:, right] + zb[1, :, right].astype(F32)).astype(BF16)
        zback(1, 1).start()
        zback(2, -1).wait_recv()
        zt[2] = (plane(s_a) + zb[2].astype(F32)).astype(BF16)
        zback(2, -1).start()
        zback(3, 1).wait_recv()
        zt[3] = (plane(s_b) + zb[3].astype(F32)).astype(BF16)
        zback(3, 1).start()
        for k, n in ((0, -1), (1, 1), (2, -1), (3, 1)):
            zback(k, n).wait_send()

    def last(d, k):
        to = up(d)
        if k == 0:
            src, dst = fb.at[:, pl.ds(mult(QD * to, QD), QD)], tg
        else:
            src, dst = fb.at[:, pl.ds(D, 128)], sc
        if d == 0:
            return pltpu.make_async_copy(src, dst, lr.at[k])
        return remote(src, dst, ls.at[k, d], lr.at[k], (i, to))

    @pl.when(owner)
    def _():
        for d in range(NY):
            for k in range(2):
                last(d, k).start()

    grad_pass(0)
    grad_pass(1)

    for m in (2, 0, 1):
        for h, near, far in ((0, 5, 2), (1, 3, 4)):
            arrived(rr.at[m, near], grecv.at[m, near], ys)
            arrived(rr.at[m, far], grecv.at[m, far], ys)
            fin[h] = gpart(m, 0, h)[...].astype(F32) + (rr[m, near].astype(F32) + rr[m, far].astype(F32))
            sums_ref[m, HALF * h : HALF * (h + 1), :] = fin[h].astype(sums_ref.dtype)

    arrived(tg, lr.at[0], ys)
    arrived(sc, lr.at[1], ys)
    tgrad_ref[...] = tg[...]
    known = sc[:, 0:EXPERTS].astype(F32) + sc[:, EXPERTS:].astype(F32)
    expert = lax.broadcasted_iota(jnp.int32, (TOK, EXPERTS), 1)
    for k in range(8):
        same = expert == routes_ref[:, k : k + 1]
        rgrad_ref[:, k : k + 1] = jnp.sum(jnp.where(same, known, 0.0), axis=1, keepdims=True)

    @pl.when(jnp.logical_not(owner))
    def _():
        sent(stage, ys, yr.at[0])

    @pl.when(owner)
    def _():
        for d in range(1, NY):
            for k in range(2):
                last(d, k).wait_send()

    for m in range(3):
        for n in range(2):
            for k in range(3):
                sent(wpart(m, 0, 0), ws.at[m, n, k], wr.at[m, 0, 0])
        for k in range(6):
            sent(rr.at[m, k], gsend.at[m, k], grecv.at[m, k])

    @pl.when(jnp.logical_and(column, jnp.logical_not(odd)))
    def _():
        for f in range(5):
            for k in range(2):
                for n in (1, -1):
                    zcopy(n, s_own, f, k).wait_send()

    @pl.when(jnp.logical_and(column, odd))
    def _():
        for f in range(5):
            for n in (1, -1):
                zcopy(n, s_own, f, 0).wait_send()
            zcopy(1 if f in (4, 0, 1) else -1, s_own, f, 1).wait_send()

    @pl.when(column)
    def _():
        for pair in range(2):
            for d in range(1, 8):
                sent(rowpart(0, 0), xs.at[pair, d], xr.at[0, 0])

    for pair in range(2):
        for d in range(1, NX):
            back_send(d, pair).wait_send()

        @pl.when(jnp.logical_not(column))
        def _():
            back_send(0, pair).wait_send()


def exchange(tokens, cotangent, routes_t, gains_t, routes, w_gate, w_up, w_down):
    vmem = pl.BlockSpec(memory_space=pltpu.VMEM)
    whole = pl.BlockSpec(memory_space=pl.ANY)
    dma = pltpu.SemaphoreType.DMA
    return pl.pallas_call(
        kernel,
        out_shape=(
            jax.ShapeDtypeStruct((3, HID, D), BF16),
            jax.ShapeDtypeStruct((TOK, QD), BF16),
            jax.ShapeDtypeStruct((TOK, 8), F32),
        ),
        in_specs=[vmem] * 5 + [whole] * 3,
        out_specs=(vmem, vmem, vmem),
        scratch_shapes=[
            pltpu.VMEM((3, FF, D), BF16),
            pltpu.VMEM((3, FF, D), BF16),
            pltpu.VMEM((3, 6, HALF, D), BF16),
            pltpu.VMEM((2, NY, 2 * TOK, 2 * QD), BF16),
            pltpu.VMEM((4, 2 * EXPERTS, TOK), F32),
            pltpu.VMEM((2, 8 * PAIR, WIDE), BF16),
            pltpu.VMEM((ROWS, WIDE), BF16),
            pltpu.VMEM((2, 8 * PAIR, 2 * TOK), BF16),
            pltpu.VMEM((3, ROWS, 256), F32),
            pltpu.VMEM((3, ROWS, 256), F32),
            pltpu.VMEM((ROWS, 1), F32),
            pltpu.VMEM((3, ROWS, 256), BF16),
            pltpu.VMEM((3, ROWS, 256), BF16),
            pltpu.VMEM((ROWS, BACK), BF16),
            pltpu.VMEM((2, 8 * PAIR, BACK), BF16),
            pltpu.VMEM((2, 2 * TOK, BACK), F32),
            pltpu.VMEM((4, TOK, BACK), BF16),
            pltpu.VMEM((4, TOK, BACK), BF16),
            pltpu.VMEM((TOK, BACK), BF16),
            pltpu.VMEM((TOK, 2 * QD), BF16),
            pltpu.VMEM((TOK, QD), BF16),
            pltpu.VMEM((TOK, 128), BF16),
            pltpu.VMEM((2, HALF, D), F32),
            dma((3, 2, 3)),
            dma((3, 2, 3)),
            dma((3,)),
            dma((3, 6)),
            dma((3, 6)),
            dma,
            dma((NY,)),
            dma((2, 2, 5)),
            dma((4, 5)),
            dma((2, 8)),
            dma((2, NX)),
            dma((2, NX)),
            dma((2, 8)),
            dma((4,)),
            dma((4,)),
            dma((2, NY)),
            dma((2,)),
        ],
        compiler_params=pltpu.CompilerParams(
            collective_id=0, has_side_effects=True, vmem_limit_bytes=64 * 1024 * 1024 - 256 * 1024
        ),
    )(tokens, cotangent, routes_t, gains_t, routes, w_gate, w_up, w_down)


def soften(grid, latent, scale):
    level = grid.astype(F32) + 0.5 * (1.0 + jnp.tanh(latent.astype(F32) / temper))
    return (level * scale).astype(BF16)


def latent_grad(grad_weight, latent, scale):
    slope = jnp.tanh(latent.astype(F32) / temper)
    return (grad_factor * grad_weight.astype(F32) * scale * (1.0 - slope * slope) / (2.0 * temper))[None]


def body(
    tokens, cotangent, route_weights, routes,
    grid_gate, latent_gate, scale_gate,
    grid_up, latent_up, scale_up,
    grid_down, latent_down, scale_down,
):
    rows_g, rows_u, cols_d = scale_gate[0][:, None], scale_up[0][:, None], scale_down[0][None, :]
    sums, token_grad, route_grad = exchange(
        tokens, cotangent, routes.T, route_weights.astype(F32).T, routes,
        soften(grid_gate[0], latent_gate[0], rows_g),
        soften(grid_up[0], latent_up[0], rows_u),
        soften(grid_down[0], latent_down[0], cols_d),
    )
    return (
        latent_grad(sums[0], latent_gate[0], rows_g),
        latent_grad(sums[1], latent_up[0], rows_u),
        latent_grad(sums[2], latent_down[0], cols_d),
        token_grad,
        route_grad,
    )


def solution(mesh):
    return jax.shard_map(
        body,
        mesh=mesh,
        in_specs=(
            P("ep", "tp"), P("ep", "tp"), P("ep", None), P("ep", None),
            P("ep", "tp", None), P("ep", "tp", None), P("ep", "tp"),
            P("ep", "tp", None), P("ep", "tp", None), P("ep", "tp"),
            P("ep", "tp", None), P("ep", "tp", None), P("ep", None),
        ),
        out_specs=(
            P("ep", "tp", None), P("ep", "tp", None), P("ep", "tp", None), P("ep", "tp"), P("ep", None),
        ),
        check_vma=False,
    )
```

```python
import jax
import jax.numpy as jnp
from jax import lax
from jax.experimental import pallas as pl
from jax.experimental.pallas import tpu as pltpu
from jax.sharding import PartitionSpec as P

temper = 0.25
grad_factor = 8.0

NZ, NX, NY = 8, 4, 4
D, FF, TOK, EXPERTS, CAP = 2048, 768, 128, 64, 24
QD = D // NY
HID = FF // NY
HH = 2 * HID
SRC = 4 * CAP
ROWS = NX * SRC
EXTRA = 128
F32, BF16 = jnp.float32, jnp.bfloat16
MESH = pl.DeviceIdType.MESH


def dot_nt(a, b):
    return lax.dot_general(a, b, (((1,), (1,)), ((), ())), preferred_element_type=F32)


def dot_nn(a, b):
    return lax.dot_general(a, b, (((1,), (0,)), ((), ())), preferred_element_type=F32)


ORDER = (0, 1, 3, 2)


def going(f, h):
    at = EXTRA + 2 * QD * f + QD * h
    return slice(at, at + QD)


def lanes_of(f):
    return pl.ds(pl.multiple_of(EXTRA + 2 * QD * f, 128), 2 * QD)


def coming(f):
    return slice(QD * f, QD * (f + 1) + (EXTRA if f == NY - 1 else 0))


def feature(f):
    return slice(QD * f, QD * (f + 1))


def kernel(
    tok_ref, cot_ref, rt_ref, wt_ref, gg_ref, lg_ref, gu_ref, lu_ref, gd_ref, ld_ref, sg_ref, su_ref, sd_ref,
    og_ref, ou_ref, od_ref, tgrad_ref, rgrad_ref,
    raw, wf, grad, rr, blk, aux, sendbuf, rows, smat, smt, gs, us, bh, sco, dg, du, lt,
    bown, bsend, bgot, br, rb, part, zb, zt, fb, stage, tg, sc,
    rawsem, ws, wr, gsend, grecv, ys, yr, zs, zr, xs, xr, fs, fr, es, er, bs, brr, zbs, zbr, ls, lr,
):
    i, y = lax.axis_index("ep"), lax.axis_index("tp")
    z, x, c = i // 8, lax.rem(i, 8) // 2, lax.rem(i, 2)
    own = 2 * x + c
    column = c == y // 2
    odd = lax.rem(z + y, 2) == 1
    source = jnp.logical_and(column, jnp.logical_not(odd))
    relay = jnp.logical_and(column, odd)
    yb = 2 * c + lax.rem(z, 2)
    owner = y == yb
    flip, mirror = y + 1 - 2 * lax.rem(y, 2), NY - 1 - y
    wpair = flip * (1 - c) + mirror * c
    rpair = mirror * (1 - c) + flip * c

    def up(n):
        return lax.rem(y + n + NY, NY)

    def zat(n):
        return lax.rem(z + n + NZ, NZ)

    def zdev(n):
        return (8 * zat(n) + own, y)

    def remote(src, dst, send, recv, dev):
        return pltpu.make_async_remote_copy(
            src_ref=src, dst_ref=dst, send_sem=send, recv_sem=recv, device_id=dev, device_id_type=MESH
        )

    def arrived(dst, recv):
        remote(dst, dst, ys, recv, (i, up(1))).wait_recv()

    def sent(src, send):
        remote(src, src, send, yr.at[0], (i, up(1))).wait_send()

    raws = ((gg_ref, lg_ref), (gu_ref, lu_ref), (gd_ref, ld_ref))
    for m in range(3):
        for k in range(2):
            pltpu.make_async_copy(raws[m][k], raw.at[m, k], rawsem.at[m, k]).start()

    barrier = pltpu.get_barrier_semaphore()
    for d in range(1, NY):
        pl.semaphore_signal(barrier, inc=1, device_id=(i, up(d)), device_id_type=MESH)
    for d in (1, -1, 2, -2, 3, -3):
        pl.semaphore_signal(barrier, inc=1, device_id=zdev(d), device_id_type=MESH)
    for d in range(1, 8):
        pl.semaphore_signal(barrier, inc=1, device_id=(8 * z + lax.rem(own + d, 8), y), device_id_type=MESH)

    stage[:, 0:QD] = tok_ref[...]
    stage[:, QD:] = cot_ref[...]
    s_own = z // 2
    order = [up(d) for d in ORDER]

    def block(s, f):
        return blk.at[f, pl.ds(pl.multiple_of(TOK * s, TOK), TOK), :]

    @pl.when(owner)
    def _():
        expert = lax.broadcasted_iota(jnp.int32, (EXPERTS, TOK), 0)
        hit = jnp.zeros((EXPERTS, TOK), F32)
        weight = jnp.zeros((EXPERTS, TOK), F32)
        gains = wt_ref[...].astype(F32)
        for k in range(8):
            same = expert == rt_ref[k : k + 1, :]
            hit = hit + jnp.where(same, 1.0, 0.0)
            weight = weight + jnp.where(same, gains[k : k + 1, :], 0.0)
        before = lax.broadcasted_iota(jnp.int32, (TOK, TOK), 0) < lax.broadcasted_iota(jnp.int32, (TOK, TOK), 1)
        slot = dot_nn(hit.astype(BF16), jnp.where(before, 1.0, 0.0).astype(BF16))
        aux[s_own, 0:EXPERTS, :] = jnp.where(hit > 0.0, slot, -1000.0)
        aux[s_own, EXPERTS:, :] = weight

    pl.semaphore_wait(barrier, 3 + 6 + 7)

    @pl.when(jnp.logical_not(owner))
    def _():
        remote(stage, block(s_own, y), ys, yr.at[y], (i, yb)).start()

    def piece(s, f):
        return aux.at[s] if f is None else block(s, f)

    def zcopy(n, s, f):
        at = 4 if f is None else f
        return remote(piece(s, f), piece(s, f), zs.at[int(n < 0), abs(n) - 1, at], zr.at[s, at], zdev(n))

    def zgot(s, f):
        arrived(piece(s, f), zr.at[s, 4 if f is None else f])

    def give(f):
        zcopy(1, s_own, f).start()
        zcopy(-1, s_own, f).start()

    def both(k):
        return (None, order[0]) if k == 0 else (order[k],)

    @pl.when(source)
    def _():
        block(s_own, y)[...] = stage[...]
        give(None)
        give(y)

    diagonal = lax.broadcasted_iota(jnp.int32, (HID, HID), 0) == lax.broadcasted_iota(jnp.int32, (HID, HID), 1)

    def column_of(ref):
        return jnp.sum(jnp.where(diagonal, ref[...], 0.0), axis=1, keepdims=True)

    sco[0, 0:HID, :] = column_of(sg_ref)
    sco[1, 0:HID, :] = column_of(su_ref)

    def scale_of(m, at, n):
        return sd_ref[...] if m == 2 else sco[m, pl.ds(at, n), :]

    def wcopy(m):
        return remote(wf.at[m, 0:HID, :], wf.at[m, HID:HH, :], ws.at[m], wr.at[m], (i, wpair))

    def soften(m):
        for k in range(2):
            pltpu.make_async_copy(raws[m][k], raw.at[m, k], rawsem.at[m, k]).wait()

        @pl.loop(0, HID // 16)
        def _(t):
            at = pl.multiple_of(16 * t, 16)
            grid = raw[m, 0, pl.ds(at, 16), :].astype(F32)
            latent = raw[m, 1, pl.ds(at, 16), :].astype(F32)
            level = grid + 0.5 * (1.0 + jnp.tanh(latent / temper))
            wf[m, pl.ds(at, 16), :] = (level * scale_of(m, at, 16)).astype(BF16)

        wcopy(m).start()

    soften(0)
    soften(1)
    soften(2)

    @pl.when(source)
    def _():
        for f in order[1:]:
            arrived(block(s_own, f), yr.at[f])
            give(f)

    def relay_piece(k):
        for f in both(k):
            zgot(zat(-1) // 2, f)
            zcopy(1, zat(-1) // 2, f).start()
            zcopy(2, zat(-1) // 2, f).start()
            if k < 2:
                zcopy(3, zat(-1) // 2, f).start()
            zgot(zat(1) // 2, f)
            zcopy(-1, zat(1) // 2, f).start()
            zcopy(-2, zat(1) // 2, f).start()
            if k >= 2:
                zcopy(-3, zat(1) // 2, f).start()

    @pl.when(relay)
    def _():
        relay_piece(0)
        relay_piece(1)

    def rowpart(xsrc, lanes):
        return rows.at[pl.ds(pl.multiple_of(SRC * xsrc, SRC), SRC), lanes]

    def out_lanes(k):
        return slice(0, EXTRA) if k == NY else lanes_of(order[k])

    def row_send(d, k):
        j = lax.rem(own + d, 8)
        src = sendbuf.at[pl.ds(pl.multiple_of(SRC * j, SRC), SRC), out_lanes(k)]
        if d == 0:
            return pltpu.make_async_copy(src, rowpart(x, out_lanes(k)), xr.at[k, x])
        return remote(src, rowpart(x, out_lanes(k)), xs.at[k, d], xr.at[k, x], (8 * z + j, y))

    def swap_rows(k):
        return remote(
            rows.at[0:ROWS, out_lanes(k)], rows.at[ROWS : 2 * ROWS, out_lanes(k)], fs.at[k], fr.at[k], (i, rpair)
        )

    def with_extra(k):
        return (NY, 0) if k == 0 else (k,)

    def forward(k):
        for g in with_extra(k):
            for xsrc in range(NX):
                arrived(rowpart(xsrc, out_lanes(g)), xr.at[g, xsrc])
            swap_rows(g).start()

    for k in range(NY):

        @pl.when(source)
        def _():
            for f in both(k):
                for n in (2, -2, 4):
                    zgot(zat(n) // 2, f)

        @pl.when(relay)
        def _():
            for f in both(k):
                for n in (3, -3):
                    zgot(zat(n) // 2, f)

        @pl.when(column)
        def _():
            if k == 0:
                slots = [aux[s, pl.ds(pl.multiple_of(8 * z, 8), 8), :] + float(CAP * s) for s in range(4)]
                gains = [aux[s, pl.ds(pl.multiple_of(EXPERTS + 8 * z, 8), 8), :] for s in range(4)]
                slots, gains = jnp.concatenate(slots, axis=1), jnp.concatenate(gains, axis=1)
                place = lax.broadcasted_iota(jnp.int32, (SRC, 4 * TOK), 0).astype(F32)
                for j in range(8):
                    chosen = place == slots[j : j + 1, :]
                    smat[SRC * j : SRC * (j + 1), :] = jnp.where(chosen, 1.0, 0.0).astype(BF16)
                    gain = jnp.sum(jnp.where(chosen, gains[j : j + 1, :], 0.0), axis=1, keepdims=True)
                    sendbuf[SRC * j : SRC * (j + 1), 0:EXTRA] = jnp.broadcast_to(gain, (SRC, EXTRA)).astype(BF16)
            f = order[k]
            for h in range(2):
                picked = dot_nn(smat[...], blk[f, :, QD * h : QD * (h + 1)])
                sendbuf[:, pl.ds(pl.multiple_of(EXTRA + 2 * QD * f + QD * h, 128), QD)] = picked.astype(BF16)
            for g in with_extra(k):
                for d in range(8):
                    row_send(d, g).start()

        @pl.when(relay)
        def _():
            if k + 2 < NY:
                relay_piece(k + 2)

        if k >= 1:
            forward(k - 1)
    forward(NY - 1)

    @pl.when(column)
    def _():
        for t in range(4):
            lanes = slice(TOK * t, TOK * (t + 1))
            smt[lanes, :] = smat[:, lanes].astype(F32).T.astype(BF16)

    for m in range(3):
        wcopy(m).wait_recv()

    def hidden(r):
        part_rows = slice(ROWS * r, ROWS * (r + 1))
        for out, m, h in ((gs, 0, 0), (us, 1, 0), (bh, 2, 1)):
            total = None
            for f in range(NY):
                term = dot_nt(rows[part_rows, going(f, h)], wf[m, :, feature(f)])
                total = term if total is None else total + term
            out[...] = total

        @pl.loop(0, ROWS // 128)
        def _(t):
            at = pl.multiple_of(128 * t, 128)
            here = pl.ds(at, 128)
            g, u, back = gs[here, :], us[here, :], bh[here, :]
            weight = rows[pl.ds(pl.multiple_of(ROWS * r + at, 128), 128), 0:EXTRA][:, 0:1].astype(F32)
            sigma = jax.nn.sigmoid(g)
            active = g * sigma
            value = active * u
            score = jnp.sum(value * back, axis=1, keepdims=True)
            delta = back * weight
            there = pl.ds(pl.multiple_of(ROWS * r + at, 128), 128)
            d_gate = delta * u * sigma * (1.0 + g * (1.0 - sigma))
            d_up = delta * active
            dg[here, :] = d_gate.astype(BF16)
            du[here, :] = d_up.astype(BF16)
            sco[2 + r, here, :] = score
            lt[0, :, there] = d_gate.T.astype(BF16)
            lt[1, :, there] = d_up.T.astype(BF16)
            lt[2, :, there] = (value * weight).T.astype(BF16)

    def back_of(f):
        return dot_nn(dg[...], wf[0, :, feature(f)]) + dot_nn(du[...], wf[1, :, feature(f)])

    lane = lax.broadcasted_iota(jnp.int32, (ROWS, EXTRA), 1)

    def split(score):
        high = score.astype(BF16).astype(F32)
        spread = jnp.where(lane == i, high, 0.0) + jnp.where(lane == i + EXPERTS, score - high, 0.0)
        return spread.astype(BF16)

    def swap_back(f):
        return remote(bsend.at[:, coming(f)], bgot.at[:, coming(f)], es.at[f], er.at[f], (i, rpair))

    hidden(0)
    for f in range(NY):
        bown[:, feature(f)] = back_of(f)
    for k in range(NY + 1):
        lanes = slice(0, EXTRA) if k == NY else lanes_of(lax.rem(rpair + ORDER[k], NY))
        arrived(rows.at[ROWS : 2 * ROWS, lanes], fr.at[k])
    hidden(1)
    for f in range(NY):
        bsend[:, feature(f)] = back_of(f).astype(BF16)
        if f == NY - 1:
            score = sco[3, :, :]
            high = score.astype(BF16).astype(F32)
            spread = jnp.where(lane == 0, high, 0.0) + jnp.where(lane == 1, score - high, 0.0)
            bsend[:, D:] = spread.astype(BF16)
        swap_back(f).start()

    def gcopy(m):
        return remote(grad.at[m, HID:HH, :], rr.at[m], gsend.at[m], grecv.at[m], (i, wpair))

    def outer(m):
        h = 1 if m == 2 else 0
        for f in range(NY):
            grad[m, :, feature(f)] = dot_nn(lt[m], rows[:, going(f, h)]).astype(BF16)

    def back_send(d, f):
        xsrc = lax.rem(x + d, NX)
        return remote(
            br.at[pl.ds(pl.multiple_of(SRC * xsrc, SRC), SRC), coming(f)],
            rb.at[pl.ds(pl.multiple_of(SRC * own, SRC), SRC), coming(f)],
            bs.at[f, d], brr.at[f, own], (8 * z + 2 * xsrc + y // 2, y),
        )

    def give_back(f):
        swap_back(f).wait_recv()
        br[:, feature(f)] = (bown[:, feature(f)] + bgot[:, feature(f)].astype(F32)).astype(BF16)
        if f == NY - 1:
            other = bgot[:, D:].astype(F32)
            br[:, D:] = split(sco[2, :, :] + (other[:, 0:1] + other[:, 1:2]))
        for d in range(1, NX):
            back_send(d, f).start()

        @pl.when(column)
        def _():
            pltpu.make_async_copy(
                br.at[pl.ds(pl.multiple_of(SRC * x, SRC), SRC), coming(f)],
                rb.at[pl.ds(pl.multiple_of(SRC * own, SRC), SRC), coming(f)], brr.at[f, own],
            ).start()

        @pl.when(jnp.logical_not(column))
        def _():
            back_send(0, f).start()

    def plane(s, f):
        return part.at[pl.ds(pl.multiple_of(TOK * s, TOK), TOK), coming(f)]

    def zback(src, n, slot, f):
        return remote(src, zb.at[slot, :, coming(f)], zbs.at[f, slot], zbr.at[f, slot], zdev(n))

    def got(slot, f):
        arrived(zb.at[slot, :, coming(f)], zbr.at[f, slot])
        return zb[slot, :, coming(f)].astype(F32)

    def mine(n, f):
        return plane(zat(n) // 2, f)

    def combine(f):
        for j in range(8):
            arrived(rb.at[pl.ds(SRC * j, SRC), coming(f)], brr.at[f, j])
        part[:, coming(f)] = dot_nn(smt[...], rb[:, coming(f)]).astype(BF16)

    def last(f):
        @pl.when(y == f)
        def _():
            pltpu.make_async_copy(fb.at[:, feature(f)], tg, lr.at[0]).start()

        @pl.when(y != f)
        def _():
            remote(fb.at[:, feature(f)], tg, ls.at[f], lr.at[0], (i, f)).start()

    def last_score(d):
        src = fb.at[:, D:]
        if d == 0:
            return pltpu.make_async_copy(src, sc, lr.at[1])
        return remote(src, sc, ls.at[NY + d], lr.at[1], (i, up(d)))

    def one(f):
        @pl.when(column)
        def _():
            combine(f)

        @pl.when(source)
        def _():
            zback(mine(-2, f), -1, 0, f).start()
            zback(mine(2, f), 1, 1, f).start()
            zback(mine(4, f), -3 if f < 2 else 3, 4, f).start()

        @pl.when(relay)
        def _():
            zback(mine(-3, f), -2, 2, f).start()
            zback(mine(3, f), 2, 3, f).start()

    def two(f):
        @pl.when(relay)
        def _():
            for side, n in ((0, -1), (1, 1)):
                total = mine(n, f)[...].astype(F32) + (got(side, f) + got(2 + side, f))
                if (f < 2) == (side == 0):
                    total = total + got(4, f)
                zt[side, :, coming(f)] = total.astype(BF16)
                zback(zt.at[side, :, coming(f)], n, side, f).start()

    def three(f):
        @pl.when(source)
        def _():
            fb[:, coming(f)] = (mine(0, f)[...].astype(F32) + (got(0, f) + got(1, f))).astype(BF16)
            last(f)
            if f == NY - 1:
                for d in range(NY):
                    last_score(d).start()

    outer(2)
    give_back(0)
    outer(0)
    give_back(1)
    one(0)
    outer(1)
    give_back(2)
    one(1)
    two(0)
    give_back(3)
    for m in (2, 0, 1):
        gcopy(m).start()
    one(2)
    two(1)
    three(0)
    one(3)
    two(2)
    three(1)
    two(3)
    three(2)
    three(3)

    def finish(m, out):
        gcopy(m).wait_recv()

        @pl.loop(0, HID // 16)
        def _(t):
            at = pl.multiple_of(16 * t, 16)
            here = pl.ds(at, 16)
            slope = jnp.tanh(raw[m, 1, here, :].astype(F32) / temper)
            total = grad[m, here, :].astype(F32) + rr[m, here, :].astype(F32)
            value = grad_factor * total * scale_of(m, at, 16) * (1.0 - slope * slope) / (2.0 * temper)
            out[here, :] = value.astype(BF16)

    finish(2, od_ref)
    finish(0, og_ref)
    finish(1, ou_ref)

    arrived(tg, lr.at[0])
    arrived(sc, lr.at[1])
    tgrad_ref[...] = tg[...]
    turned = sc[...].astype(F32).T
    known = turned[0:EXPERTS, :] + turned[EXPERTS:, :]
    expert = lax.broadcasted_iota(jnp.int32, (EXPERTS, TOK), 0)
    for k in range(8):
        same = expert == rt_ref[k : k + 1, :]
        rgrad_ref[k : k + 1, :] = jnp.sum(jnp.where(same, known, 0.0), axis=0, keepdims=True)

    @pl.when(jnp.logical_not(owner))
    def _():
        sent(stage, ys)

    @pl.when(owner)
    def _():
        for d in range(1, NY):
            last_score(d).wait_send()
        for f in range(NY):

            @pl.when(y != f)
            def _():
                sent(tg, ls.at[f])

    for m in range(3):
        wcopy(m).wait_send()
        gcopy(m).wait_send()
    for k in range(NY + 1):
        swap_rows(k).wait_send()

        @pl.when(column)
        def _():
            for d in range(1, 8):
                row_send(d, k).wait_send()

    for f in range(NY):
        swap_back(f).wait_send()
        for d in range(1, NX):
            back_send(d, f).wait_send()

        @pl.when(jnp.logical_not(column))
        def _():
            back_send(0, f).wait_send()

        @pl.when(column)
        def _():
            for slot in range(2):
                zback(mine(0, f), 1, slot, f).wait_send()

        @pl.when(source)
        def _():
            zback(mine(0, f), 1, 4, f).wait_send()

        @pl.when(relay)
        def _():
            for slot in range(2, 4):
                zback(mine(0, f), 1, slot, f).wait_send()

    for k in range(NY):
        for f in both(k):

            @pl.when(source)
            def _():
                for n in (1, -1):
                    zcopy(n, s_own, f).wait_send()

            @pl.when(relay)
            def _():
                for n in (1, -1, 2, -2, 3 if k < 2 else -3):
                    zcopy(n, s_own, f).wait_send()


def exchange(*operands):
    vmem = pl.BlockSpec(memory_space=pltpu.VMEM)
    whole = pl.BlockSpec(memory_space=pl.ANY)
    dma = pltpu.SemaphoreType.DMA
    return pl.pallas_call(
        kernel,
        out_shape=(
            jax.ShapeDtypeStruct((HID, D), BF16),
            jax.ShapeDtypeStruct((HID, D), BF16),
            jax.ShapeDtypeStruct((HID, D), BF16),
            jax.ShapeDtypeStruct((TOK, QD), BF16),
            jax.ShapeDtypeStruct((8, TOK), F32),
        ),
        in_specs=[vmem] * 4 + [whole] * 6 + [vmem] * 3,
        out_specs=(vmem,) * 5,
        scratch_shapes=[
            pltpu.VMEM((3, 2, HID, D), BF16),
            pltpu.VMEM((3, HH, D), BF16),
            pltpu.VMEM((3, HH, D), BF16),
            pltpu.VMEM((3, HID, D), BF16),
            pltpu.VMEM((NY, 4 * TOK, 2 * QD), BF16),
            pltpu.VMEM((4, 2 * EXPERTS, TOK), F32),
            pltpu.VMEM((8 * SRC, 2 * D + EXTRA), BF16),
            pltpu.VMEM((2 * ROWS, 2 * D + EXTRA), BF16),
            pltpu.VMEM((8 * SRC, 4 * TOK), BF16),
            pltpu.VMEM((4 * TOK, 8 * SRC), BF16),
            pltpu.VMEM((ROWS, HH), F32),
            pltpu.VMEM((ROWS, HH), F32),
            pltpu.VMEM((ROWS, HH), F32),
            pltpu.VMEM((4, ROWS, 1), F32),
            pltpu.VMEM((ROWS, HH), BF16),
            pltpu.VMEM((ROWS, HH), BF16),
            pltpu.VMEM((3, HH, 2 * ROWS), BF16),
            pltpu.VMEM((ROWS, D), F32),
            pltpu.VMEM((ROWS, D + EXTRA), BF16),
            pltpu.VMEM((ROWS, D + EXTRA), BF16),
            pltpu.VMEM((ROWS, D + EXTRA), BF16),
            pltpu.VMEM((8 * SRC, D + EXTRA), BF16),
            pltpu.VMEM((4 * TOK, D + EXTRA), BF16),
            pltpu.VMEM((5, TOK, D + EXTRA), BF16),
            pltpu.VMEM((2, TOK, D + EXTRA), BF16),
            pltpu.VMEM((TOK, D + EXTRA), BF16),
            pltpu.VMEM((TOK, 2 * QD), BF16),
            pltpu.VMEM((TOK, QD), BF16),
            pltpu.VMEM((TOK, EXTRA), BF16),
            dma((3, 2)),
            dma((3,)),
            dma((3,)),
            dma((3,)),
            dma((3,)),
            dma,
            dma((NY,)),
            dma((2, 3, 5)),
            dma((4, 5)),
            dma((NY + 1, 8)),
            dma((NY + 1, NX)),
            dma((NY + 1,)),
            dma((NY + 1,)),
            dma((NY,)),
            dma((NY,)),
            dma((NY, NX)),
            dma((NY, 8)),
            dma((NY, 5)),
            dma((NY, 5)),
            dma((2 * NY,)),
            dma((2,)),
        ],
        compiler_params=pltpu.CompilerParams(
            collective_id=0, has_side_effects=True, vmem_limit_bytes=64 * 1024 * 1024 - 256 * 1024
        ),
    )(*operands)


def body(
    tokens, cotangent, route_weights, routes,
    grid_gate, latent_gate, scale_gate,
    grid_up, latent_up, scale_up,
    grid_down, latent_down, scale_down,
):
    grad_gate, grad_up, grad_down, token_grad, route_grad = exchange(
        tokens, cotangent, routes.T, route_weights.T,
        grid_gate[0], latent_gate[0], grid_up[0], latent_up[0], grid_down[0], latent_down[0],
        scale_gate, scale_up, scale_down,
    )
    return (
        grad_gate.astype(F32)[None], grad_up.astype(F32)[None], grad_down.astype(F32)[None],
        token_grad, route_grad.T,
    )


def solution(mesh):
    return jax.shard_map(
        body,
        mesh=mesh,
        in_specs=(
            P("ep", "tp"), P("ep", "tp"), P("ep", None), P("ep", None),
            P("ep", "tp", None), P("ep", "tp", None), P("ep", "tp"),
            P("ep", "tp", None), P("ep", "tp", None), P("ep", "tp"),
            P("ep", "tp", None), P("ep", "tp", None), P("ep", None),
        ),
        out_specs=(
            P("ep", "tp", None), P("ep", "tp", None), P("ep", "tp", None), P("ep", "tp"), P("ep", None),
        ),
        check_vma=False,
    )
```

```python
import jax
import jax.numpy as jnp
from jax import lax
from jax.experimental import pallas as pl
from jax.experimental.pallas import tpu as pltpu
from jax.sharding import PartitionSpec as P

temper = 0.25
grad_factor = 8.0

NZ, NX, NY = 8, 4, 4
D, FF, TOK, EXPERTS, CAP = 2048, 768, 128, 64, 24
QD = D // NY
HID = FF // NY
HH = 2 * HID
SRC = 4 * CAP
ROWS = NX * SRC
EXTRA = 128
F32, BF16 = jnp.float32, jnp.bfloat16
MESH = pl.DeviceIdType.MESH


def dot_nt(a, b):
    return lax.dot_general(a, b, (((1,), (1,)), ((), ())), preferred_element_type=F32)


def dot_nn(a, b):
    return lax.dot_general(a, b, (((1,), (0,)), ((), ())), preferred_element_type=F32)


ORDER = (0, 1, 3, 2)
PIECES = 2 * NY
AHEAD = 2


def going(f, h):
    at = EXTRA + 2 * QD * f + QD * h
    return slice(at, at + QD)


def lanes_of(f, h):
    return pl.ds(pl.multiple_of(EXTRA + 2 * QD * f + QD * h, 128), QD)


def coming(f):
    return slice(QD * f, QD * (f + 1) + (EXTRA if f == NY - 1 else 0))


def feature(f):
    return slice(QD * f, QD * (f + 1))


def kernel(
    tok_ref, cot_ref, rt_ref, wt_ref, gg_ref, lg_ref, gu_ref, lu_ref, gd_ref, ld_ref, sg_ref, su_ref, sd_ref,
    og_ref, ou_ref, od_ref, tgrad_ref, rgrad_ref,
    raw, wf, grad, rr, blk, aux, sendbuf, rows, smat, smt, gs, us, bh, sco, dg, du, lt,
    bown, bsend, bgot, br, rb, part, zb, zt, fb, tg, sc,
    rawsem, ws, wr, gsend, grecv, ys, yr, zs, zr, xs, xr, fs, fr, es, er, bs, brr, zbs, zbr, ls, lr,
):
    i, y = lax.axis_index("ep"), lax.axis_index("tp")
    z, x, c = i // 8, lax.rem(i, 8) // 2, lax.rem(i, 2)
    own = 2 * x + c
    column = c == y // 2
    odd = lax.rem(z + y, 2) == 1
    source = jnp.logical_and(column, jnp.logical_not(odd))
    relay = jnp.logical_and(column, odd)
    yb = 2 * c + lax.rem(z, 2)
    owner = y == yb
    flip, mirror = y + 1 - 2 * lax.rem(y, 2), NY - 1 - y
    wpair = flip * (1 - c) + mirror * c
    rpair = mirror * (1 - c) + flip * c

    def up(n):
        return lax.rem(y + n + NY, NY)

    def zat(n):
        return lax.rem(z + n + NZ, NZ)

    def zdev(n):
        return (8 * zat(n) + own, y)

    def remote(src, dst, send, recv, dev):
        return pltpu.make_async_remote_copy(
            src_ref=src, dst_ref=dst, send_sem=send, recv_sem=recv, device_id=dev, device_id_type=MESH
        )

    def arrived(dst, recv):
        remote(dst, dst, ys.at[0], recv, (i, up(1))).wait_recv()

    def sent(src, send):
        remote(src, src, send, yr.at[0, 0], (i, up(1))).wait_send()

    raws = ((gg_ref, lg_ref), (gu_ref, lu_ref), (gd_ref, ld_ref))
    for m in range(3):
        for k in range(2):
            pltpu.make_async_copy(raws[m][k], raw.at[m, k], rawsem.at[m, k]).start()

    barrier = pltpu.get_barrier_semaphore()
    for d in range(1, NY):
        pl.semaphore_signal(barrier, inc=1, device_id=(i, up(d)), device_id_type=MESH)
    for d in (1, -1, 2, -2, 3, -3):
        pl.semaphore_signal(barrier, inc=1, device_id=zdev(d), device_id_type=MESH)
    for d in range(1, 8):
        pl.semaphore_signal(barrier, inc=1, device_id=(8 * z + lax.rem(own + d, 8), y), device_id_type=MESH)

    s_own = z // 2
    order = [up(d) for d in ORDER]

    def block(s, f):
        return blk.at[f, pl.ds(pl.multiple_of(TOK * s, TOK), TOK), :]

    @pl.when(owner)
    def _():
        expert = lax.broadcasted_iota(jnp.int32, (EXPERTS, TOK), 0)
        hit = jnp.zeros((EXPERTS, TOK), F32)
        weight = jnp.zeros((EXPERTS, TOK), F32)
        gains = wt_ref[...].astype(F32)
        for k in range(8):
            same = expert == rt_ref[k : k + 1, :]
            hit = hit + jnp.where(same, 1.0, 0.0)
            weight = weight + jnp.where(same, gains[k : k + 1, :], 0.0)
        before = lax.broadcasted_iota(jnp.int32, (TOK, TOK), 0) < lax.broadcasted_iota(jnp.int32, (TOK, TOK), 1)
        slot = dot_nn(hit.astype(BF16), jnp.where(before, 1.0, 0.0).astype(BF16))
        aux[s_own, 0:EXPERTS, :] = jnp.where(hit > 0.0, slot, -1000.0)
        aux[s_own, EXPERTS:, :] = weight

    pl.semaphore_wait(barrier, 3 + 6 + 7)

    halves = ((tok_ref, slice(0, QD)), (cot_ref, slice(QD, 2 * QD)))

    def token_send(h):
        src, lanes = halves[h]
        return remote(src, block(s_own, y).at[:, lanes], ys.at[h], yr.at[y, h], (i, yb))

    def token_keep(h):
        src, lanes = halves[h]
        return pltpu.make_async_copy(src, block(s_own, y).at[:, lanes], yr.at[y, h])

    for h in range(2):

        @pl.when(jnp.logical_not(owner))
        def _():
            token_send(h).start()

        @pl.when(owner)
        def _():
            token_keep(h).start()

    def piece(s, k):
        if k == PIECES:
            return aux.at[s]
        return block(s, order[k // 2]).at[:, halves[k % 2][1]]

    def zcopy(n, s, k):
        return remote(piece(s, k), piece(s, k), zs.at[int(n < 0), abs(n) - 1, k], zr.at[s, k], zdev(n))

    def zgot(s, k):
        arrived(piece(s, k), zr.at[s, k])

    def give(k):
        zcopy(1, s_own, k).start()
        zcopy(-1, s_own, k).start()

    def with_extra(k):
        return (PIECES, 0) if k == 0 else (k,)

    @pl.when(source)
    def _():
        give(PIECES)
        for h in range(2):
            token_keep(h).wait()
            give(h)

    diagonal = lax.broadcasted_iota(jnp.int32, (HID, HID), 0) == lax.broadcasted_iota(jnp.int32, (HID, HID), 1)

    def column_of(ref):
        return jnp.sum(jnp.where(diagonal, ref[...], 0.0), axis=1, keepdims=True)

    sco[0, 0:HID, :] = column_of(sg_ref)
    sco[1, 0:HID, :] = column_of(su_ref)

    def scale_of(m, at, n):
        return sd_ref[...] if m == 2 else sco[m, pl.ds(at, n), :]

    def wcopy(m):
        return remote(wf.at[m, 0:HID, :], wf.at[m, HID:HH, :], ws.at[m], wr.at[m], (i, wpair))

    def soften(m):
        for k in range(2):
            pltpu.make_async_copy(raws[m][k], raw.at[m, k], rawsem.at[m, k]).wait()

        @pl.loop(0, HID // 16)
        def _(t):
            at = pl.multiple_of(16 * t, 16)
            grid = raw[m, 0, pl.ds(at, 16), :].astype(F32)
            latent = raw[m, 1, pl.ds(at, 16), :].astype(F32)
            level = grid + 0.5 * (1.0 + jnp.tanh(latent / temper))
            wf[m, pl.ds(at, 16), :] = (level * scale_of(m, at, 16)).astype(BF16)

        wcopy(m).start()

    soften(0)
    soften(1)
    soften(2)

    def give_next(k):
        arrived(piece(s_own, k), yr.at[order[k // 2], k % 2])
        give(k)

    @pl.when(source)
    def _():
        for k in range(2, AHEAD + 2):
            give_next(k)

    def relay_piece(k):
        for n, side in ((-1, 1), (1, -1)):
            zgot(zat(n) // 2, k)
            zcopy(side, zat(n) // 2, k).start()
            zcopy(2 * side, zat(n) // 2, k).start()
            if (side == 1) == (k % 2 == 0):
                zcopy(3 * side, zat(n) // 2, k).start()

    @pl.when(relay)
    def _():
        for k in (PIECES, *range(AHEAD)):
            relay_piece(k)

    def rowpart(xsrc, lanes):
        return rows.at[pl.ds(pl.multiple_of(SRC * xsrc, SRC), SRC), lanes]

    def out_lanes(k):
        return slice(0, EXTRA) if k == PIECES else lanes_of(order[k // 2], k % 2)

    def row_send(d, k):
        j = lax.rem(own + d, 8)
        src = sendbuf.at[pl.ds(pl.multiple_of(SRC * j, SRC), SRC), out_lanes(k)]
        if d == 0:
            return pltpu.make_async_copy(src, rowpart(x, out_lanes(k)), xr.at[k, x])
        return remote(src, rowpart(x, out_lanes(k)), xs.at[k, d], xr.at[k, x], (8 * z + j, y))

    def swap_rows(k):
        return remote(
            rows.at[0:ROWS, out_lanes(k)], rows.at[ROWS : 2 * ROWS, out_lanes(k)], fs.at[k], fr.at[k], (i, rpair)
        )

    def forward(k):
        for g in with_extra(k):
            for xsrc in range(NX):
                arrived(rowpart(xsrc, out_lanes(g)), xr.at[g, xsrc])
            swap_rows(g).start()

    for k in range(PIECES):

        @pl.when(source)
        def _():
            for g in with_extra(k):
                for n in (2, -2, 4):
                    zgot(zat(n) // 2, g)

        @pl.when(relay)
        def _():
            for g in with_extra(k):
                for n in (3, -3):
                    zgot(zat(n) // 2, g)

        @pl.when(column)
        def _():
            if k == 0:
                slots = [aux[s, pl.ds(pl.multiple_of(8 * z, 8), 8), :] + float(CAP * s) for s in range(4)]
                gains = [aux[s, pl.ds(pl.multiple_of(EXPERTS + 8 * z, 8), 8), :] for s in range(4)]
                slots, gains = jnp.concatenate(slots, axis=1), jnp.concatenate(gains, axis=1)
                place = lax.broadcasted_iota(jnp.int32, (SRC, 4 * TOK), 0).astype(F32)
                for j in range(8):
                    chosen = place == slots[j : j + 1, :]
                    smat[SRC * j : SRC * (j + 1), :] = jnp.where(chosen, 1.0, 0.0).astype(BF16)
                    gain = jnp.sum(jnp.where(chosen, gains[j : j + 1, :], 0.0), axis=1, keepdims=True)
                    sendbuf[SRC * j : SRC * (j + 1), 0:EXTRA] = jnp.broadcast_to(gain, (SRC, EXTRA)).astype(BF16)
            picked = dot_nn(smat[...], blk[order[k // 2], :, halves[k % 2][1]])
            sendbuf[:, out_lanes(k)] = picked.astype(BF16)
            for g in with_extra(k):
                for d in range(8):
                    row_send(d, g).start()

        @pl.when(source)
        def _():
            if k + AHEAD + 2 < PIECES:
                give_next(k + AHEAD + 2)

        @pl.when(relay)
        def _():
            if k + AHEAD < PIECES:
                relay_piece(k + AHEAD)

        if k >= 1:
            forward(k - 1)
    forward(PIECES - 1)

    @pl.when(column)
    def _():
        for t in range(4):
            lanes = slice(TOK * t, TOK * (t + 1))
            smt[lanes, :] = smat[:, lanes].astype(F32).T.astype(BF16)

    for m in range(3):
        wcopy(m).wait_recv()

    def hidden(r):
        part_rows = slice(ROWS * r, ROWS * (r + 1))
        for out, m, h in ((gs, 0, 0), (us, 1, 0), (bh, 2, 1)):
            total = None
            for f in range(NY):
                term = dot_nt(rows[part_rows, going(f, h)], wf[m, :, feature(f)])
                total = term if total is None else total + term
            out[...] = total

        @pl.loop(0, ROWS // 128)
        def _(t):
            at = pl.multiple_of(128 * t, 128)
            here = pl.ds(at, 128)
            g, u, back = gs[here, :], us[here, :], bh[here, :]
            weight = rows[pl.ds(pl.multiple_of(ROWS * r + at, 128), 128), 0:EXTRA][:, 0:1].astype(F32)
            sigma = jax.nn.sigmoid(g)
            active = g * sigma
            value = active * u
            score = jnp.sum(value * back, axis=1, keepdims=True)
            delta = back * weight
            there = pl.ds(pl.multiple_of(ROWS * r + at, 128), 128)
            d_gate = delta * u * sigma * (1.0 + g * (1.0 - sigma))
            d_up = delta * active
            dg[here, :] = d_gate.astype(BF16)
            du[here, :] = d_up.astype(BF16)
            sco[2 + r, here, :] = score
            lt[0, :, there] = d_gate.T.astype(BF16)
            lt[1, :, there] = d_up.T.astype(BF16)
            lt[2, :, there] = (value * weight).T.astype(BF16)

    def back_of(f):
        return dot_nn(dg[...], wf[0, :, feature(f)]) + dot_nn(du[...], wf[1, :, feature(f)])

    lane = lax.broadcasted_iota(jnp.int32, (ROWS, EXTRA), 1)

    def split(score):
        high = score.astype(BF16).astype(F32)
        spread = jnp.where(lane == i, high, 0.0) + jnp.where(lane == i + EXPERTS, score - high, 0.0)
        return spread.astype(BF16)

    def swap_back(f):
        return remote(bsend.at[:, coming(f)], bgot.at[:, coming(f)], es.at[f], er.at[f], (i, rpair))

    hidden(0)
    for f in range(NY):
        bown[:, feature(f)] = back_of(f)
    for k in range(PIECES + 1):
        lanes = slice(0, EXTRA) if k == PIECES else lanes_of(lax.rem(rpair + ORDER[k // 2], NY), k % 2)
        arrived(rows.at[ROWS : 2 * ROWS, lanes], fr.at[k])
    hidden(1)
    for f in range(NY):
        bsend[:, feature(f)] = back_of(f).astype(BF16)
        if f == NY - 1:
            score = sco[3, :, :]
            high = score.astype(BF16).astype(F32)
            spread = jnp.where(lane == 0, high, 0.0) + jnp.where(lane == 1, score - high, 0.0)
            bsend[:, D:] = spread.astype(BF16)
        swap_back(f).start()

    def gcopy(m):
        return remote(grad.at[m, HID:HH, :], rr.at[m], gsend.at[m], grecv.at[m], (i, wpair))

    def outer(m):
        h = 1 if m == 2 else 0
        for f in range(NY):
            grad[m, :, feature(f)] = dot_nn(lt[m], rows[:, going(f, h)]).astype(BF16)

    def back_send(d, f):
        xsrc = lax.rem(x + d, NX)
        return remote(
            br.at[pl.ds(pl.multiple_of(SRC * xsrc, SRC), SRC), coming(f)],
            rb.at[pl.ds(pl.multiple_of(SRC * own, SRC), SRC), coming(f)],
            bs.at[f, d], brr.at[f, own], (8 * z + 2 * xsrc + y // 2, y),
        )

    def give_back(f):
        swap_back(f).wait_recv()
        br[:, feature(f)] = (bown[:, feature(f)] + bgot[:, feature(f)].astype(F32)).astype(BF16)
        if f == NY - 1:
            other = bgot[:, D:].astype(F32)
            br[:, D:] = split(sco[2, :, :] + (other[:, 0:1] + other[:, 1:2]))
        for d in range(1, NX):
            back_send(d, f).start()

        @pl.when(column)
        def _():
            pltpu.make_async_copy(
                br.at[pl.ds(pl.multiple_of(SRC * x, SRC), SRC), coming(f)],
                rb.at[pl.ds(pl.multiple_of(SRC * own, SRC), SRC), coming(f)], brr.at[f, own],
            ).start()

        @pl.when(jnp.logical_not(column))
        def _():
            back_send(0, f).start()

    def plane(s, f):
        return part.at[pl.ds(pl.multiple_of(TOK * s, TOK), TOK), coming(f)]

    def zback(src, n, slot, f):
        return remote(src, zb.at[slot, :, coming(f)], zbs.at[f, slot], zbr.at[f, slot], zdev(n))

    def got(slot, f):
        arrived(zb.at[slot, :, coming(f)], zbr.at[f, slot])
        return zb[slot, :, coming(f)].astype(F32)

    def mine(n, f):
        return plane(zat(n) // 2, f)

    def combine(f):
        for j in range(8):
            arrived(rb.at[pl.ds(SRC * j, SRC), coming(f)], brr.at[f, j])
        part[:, coming(f)] = dot_nn(smt[...], rb[:, coming(f)]).astype(BF16)

    def last(f):
        @pl.when(y == f)
        def _():
            pltpu.make_async_copy(fb.at[:, feature(f)], tg, lr.at[0]).start()

        @pl.when(y != f)
        def _():
            remote(fb.at[:, feature(f)], tg, ls.at[f], lr.at[0], (i, f)).start()

    def last_score(d):
        src = fb.at[:, D:]
        if d == 0:
            return pltpu.make_async_copy(src, sc, lr.at[1])
        return remote(src, sc, ls.at[NY + d], lr.at[1], (i, up(d)))

    def one(f):
        @pl.when(column)
        def _():
            combine(f)

        @pl.when(source)
        def _():
            zback(mine(-2, f), -1, 0, f).start()
            zback(mine(2, f), 1, 1, f).start()
            zback(mine(4, f), -3 if f < 2 else 3, 4, f).start()

        @pl.when(relay)
        def _():
            zback(mine(-3, f), -2, 2, f).start()
            zback(mine(3, f), 2, 3, f).start()

    def two(f):
        @pl.when(relay)
        def _():
            for side, n in ((0, -1), (1, 1)):
                total = mine(n, f)[...].astype(F32) + (got(side, f) + got(2 + side, f))
                if (f < 2) == (side == 0):
                    total = total + got(4, f)
                zt[side, :, coming(f)] = total.astype(BF16)
                zback(zt.at[side, :, coming(f)], n, side, f).start()

    def three(f):
        @pl.when(source)
        def _():
            fb[:, coming(f)] = (mine(0, f)[...].astype(F32) + (got(0, f) + got(1, f))).astype(BF16)
            last(f)
            if f == NY - 1:
                for d in range(NY):
                    last_score(d).start()

    outer(2)
    give_back(0)
    outer(0)
    give_back(1)
    one(0)
    outer(1)
    give_back(2)
    one(1)
    two(0)
    give_back(3)
    for m in (2, 0, 1):
        gcopy(m).start()
    one(2)
    two(1)
    three(0)
    one(3)
    two(2)
    three(1)
    two(3)
    three(2)
    three(3)

    def finish(m, out):
        gcopy(m).wait_recv()

        @pl.loop(0, HID // 16)
        def _(t):
            at = pl.multiple_of(16 * t, 16)
            here = pl.ds(at, 16)
            slope = jnp.tanh(raw[m, 1, here, :].astype(F32) / temper)
            total = grad[m, here, :].astype(F32) + rr[m, here, :].astype(F32)
            value = grad_factor * total * scale_of(m, at, 16) * (1.0 - slope * slope) / (2.0 * temper)
            out[here, :] = value.astype(BF16)

    finish(2, od_ref)
    finish(0, og_ref)
    finish(1, ou_ref)

    arrived(tg, lr.at[0])
    arrived(sc, lr.at[1])
    tgrad_ref[...] = tg[...]
    turned = sc[...].astype(F32).T
    known = turned[0:EXPERTS, :] + turned[EXPERTS:, :]
    expert = lax.broadcasted_iota(jnp.int32, (EXPERTS, TOK), 0)
    for k in range(8):
        same = expert == rt_ref[k : k + 1, :]
        rgrad_ref[k : k + 1, :] = jnp.sum(jnp.where(same, known, 0.0), axis=0, keepdims=True)

    @pl.when(jnp.logical_not(owner))
    def _():
        for h in range(2):
            token_send(h).wait_send()

    @pl.when(owner)
    def _():
        for d in range(1, NY):
            last_score(d).wait_send()
        for f in range(NY):

            @pl.when(y != f)
            def _():
                sent(tg, ls.at[f])

    for m in range(3):
        wcopy(m).wait_send()
        gcopy(m).wait_send()
    for k in range(PIECES + 1):
        swap_rows(k).wait_send()

        @pl.when(column)
        def _():
            for d in range(1, 8):
                row_send(d, k).wait_send()

    for f in range(NY):
        swap_back(f).wait_send()
        for d in range(1, NX):
            back_send(d, f).wait_send()

        @pl.when(jnp.logical_not(column))
        def _():
            back_send(0, f).wait_send()

        @pl.when(column)
        def _():
            for slot in range(2):
                zback(mine(0, f), 1, slot, f).wait_send()

        @pl.when(source)
        def _():
            zback(mine(0, f), 1, 4, f).wait_send()

        @pl.when(relay)
        def _():
            for slot in range(2, 4):
                zback(mine(0, f), 1, slot, f).wait_send()

    for k in range(PIECES + 1):

        @pl.when(source)
        def _():
            for n in (1, -1):
                zcopy(n, s_own, k).wait_send()

        @pl.when(relay)
        def _():
            for n in (1, -1, 2, -2, 3 if k % 2 == 0 else -3):
                zcopy(n, s_own, k).wait_send()


def exchange(*operands):
    vmem = pl.BlockSpec(memory_space=pltpu.VMEM)
    whole = pl.BlockSpec(memory_space=pl.ANY)
    dma = pltpu.SemaphoreType.DMA
    return pl.pallas_call(
        kernel,
        out_shape=(
            jax.ShapeDtypeStruct((HID, D), BF16),
            jax.ShapeDtypeStruct((HID, D), BF16),
            jax.ShapeDtypeStruct((HID, D), BF16),
            jax.ShapeDtypeStruct((TOK, QD), BF16),
            jax.ShapeDtypeStruct((8, TOK), F32),
        ),
        in_specs=[whole] * 2 + [vmem] * 2 + [whole] * 6 + [vmem] * 3,
        out_specs=(vmem,) * 5,
        scratch_shapes=[
            pltpu.VMEM((3, 2, HID, D), BF16),
            pltpu.VMEM((3, HH, D), BF16),
            pltpu.VMEM((3, HH, D), BF16),
            pltpu.VMEM((3, HID, D), BF16),
            pltpu.VMEM((NY, 4 * TOK, 2 * QD), BF16),
            pltpu.VMEM((4, 2 * EXPERTS, TOK), F32),
            pltpu.VMEM((8 * SRC, 2 * D + EXTRA), BF16),
            pltpu.VMEM((2 * ROWS, 2 * D + EXTRA), BF16),
            pltpu.VMEM((8 * SRC, 4 * TOK), BF16),
            pltpu.VMEM((4 * TOK, 8 * SRC), BF16),
            pltpu.VMEM((ROWS, HH), F32),
            pltpu.VMEM((ROWS, HH), F32),
            pltpu.VMEM((ROWS, HH), F32),
            pltpu.VMEM((4, ROWS, 1), F32),
            pltpu.VMEM((ROWS, HH), BF16),
            pltpu.VMEM((ROWS, HH), BF16),
            pltpu.VMEM((3, HH, 2 * ROWS), BF16),
            pltpu.VMEM((ROWS, D), F32),
            pltpu.VMEM((ROWS, D + EXTRA), BF16),
            pltpu.VMEM((ROWS, D + EXTRA), BF16),
            pltpu.VMEM((ROWS, D + EXTRA), BF16),
            pltpu.VMEM((8 * SRC, D + EXTRA), BF16),
            pltpu.VMEM((4 * TOK, D + EXTRA), BF16),
            pltpu.VMEM((5, TOK, D + EXTRA), BF16),
            pltpu.VMEM((2, TOK, D + EXTRA), BF16),
            pltpu.VMEM((TOK, D + EXTRA), BF16),
            pltpu.VMEM((TOK, QD), BF16),
            pltpu.VMEM((TOK, EXTRA), BF16),
            dma((3, 2)),
            dma((3,)),
            dma((3,)),
            dma((3,)),
            dma((3,)),
            dma((2,)),
            dma((NY, 2)),
            dma((2, 3, PIECES + 1)),
            dma((4, PIECES + 1)),
            dma((PIECES + 1, 8)),
            dma((PIECES + 1, NX)),
            dma((PIECES + 1,)),
            dma((PIECES + 1,)),
            dma((NY,)),
            dma((NY,)),
            dma((NY, NX)),
            dma((NY, 8)),
            dma((NY, 5)),
            dma((NY, 5)),
            dma((2 * NY,)),
            dma((2,)),
        ],
        compiler_params=pltpu.CompilerParams(
            collective_id=0, has_side_effects=True, vmem_limit_bytes=64 * 1024 * 1024 - 256 * 1024
        ),
    )(*operands)


def body(
    tokens, cotangent, route_weights, routes,
    grid_gate, latent_gate, scale_gate,
    grid_up, latent_up, scale_up,
    grid_down, latent_down, scale_down,
):
    grad_gate, grad_up, grad_down, token_grad, route_grad = exchange(
        tokens, cotangent, routes.T, route_weights.T,
        grid_gate[0], latent_gate[0], grid_up[0], latent_up[0], grid_down[0], latent_down[0],
        scale_gate, scale_up, scale_down,
    )
    return (
        grad_gate.astype(F32)[None], grad_up.astype(F32)[None], grad_down.astype(F32)[None],
        token_grad, route_grad.T,
    )


def solution(mesh):
    return jax.shard_map(
        body,
        mesh=mesh,
        in_specs=(
            P("ep", "tp"), P("ep", "tp"), P("ep", None), P("ep", None),
            P("ep", "tp", None), P("ep", "tp", None), P("ep", "tp"),
            P("ep", "tp", None), P("ep", "tp", None), P("ep", "tp"),
            P("ep", "tp", None), P("ep", "tp", None), P("ep", None),
        ),
        out_specs=(
            P("ep", "tp", None), P("ep", "tp", None), P("ep", "tp", None), P("ep", "tp"), P("ep", None),
        ),
        check_vma=False,
    )
```

```python
import jax
import jax.numpy as jnp
from jax import lax
from jax.experimental import pallas as pl
from jax.experimental.pallas import tpu as pltpu
from jax.sharding import PartitionSpec as P

temper = 0.25
grad_factor = 8.0

NZ, NX, NY = 8, 4, 4
D, FF, TOK, EXPERTS, CAP = 2048, 768, 128, 64, 24
QD = D // NY
HID = FF // NY
HH = 2 * HID
SRC = 4 * CAP
ROWS = NX * SRC
EXTRA = 128
F32, BF16 = jnp.float32, jnp.bfloat16
MESH = pl.DeviceIdType.MESH


def dot_nt(a, b):
    return lax.dot_general(a, b, (((1,), (1,)), ((), ())), preferred_element_type=F32)


def dot_nn(a, b):
    return lax.dot_general(a, b, (((1,), (0,)), ((), ())), preferred_element_type=F32)


ORDER = (0, 1, 3, 2)
PIECES = 2 * NY
AHEAD = 2


def going(f, h):
    at = EXTRA + 2 * QD * f + QD * h
    return slice(at, at + QD)


def lanes_of(f, h):
    return pl.ds(pl.multiple_of(EXTRA + 2 * QD * f + QD * h, 128), QD)


def coming(f):
    return slice(QD * f, QD * (f + 1) + (EXTRA if f == NY - 1 else 0))


def feature(f):
    return slice(QD * f, QD * (f + 1))


def kernel(
    tok_ref, cot_ref, rt_ref, wt_ref, gg_ref, lg_ref, gu_ref, lu_ref, gd_ref, ld_ref, sg_ref, su_ref, sd_ref,
    og_ref, ou_ref, od_ref, tgrad_ref, rgrad_ref,
    raw, wf, grad, rr, blk, aux, sendbuf, rows, smat, smt, gs, us, bh, sco, dg, du, lt,
    bown, bsend, bgot, br, rb, part, zb, zt, fb, tg, sc,
    rawsem, ws, wr, gsend, grecv, ys, yr, zs, zr, xs, xr, fs, fr, es, er, bs, brr, zbs, zbr, ls, lr,
):
    i, y = lax.axis_index("ep"), lax.axis_index("tp")
    z, x, c = i // 8, lax.rem(i, 8) // 2, lax.rem(i, 2)
    own = 2 * x + c
    column = c == y // 2
    odd = lax.rem(z + y, 2) == 1
    source = jnp.logical_and(column, jnp.logical_not(odd))
    relay = jnp.logical_and(column, odd)
    yb = 2 * c + lax.rem(z, 2)
    owner = y == yb
    flip, mirror = y + 1 - 2 * lax.rem(y, 2), NY - 1 - y
    wpair = flip * (1 - c) + mirror * c
    rpair = mirror * (1 - c) + flip * c

    def up(n):
        return lax.rem(y + n + NY, NY)

    def zat(n):
        return lax.rem(z + n + NZ, NZ)

    def zdev(n):
        return (8 * zat(n) + own, y)

    def remote(src, dst, send, recv, dev):
        return pltpu.make_async_remote_copy(
            src_ref=src, dst_ref=dst, send_sem=send, recv_sem=recv, device_id=dev, device_id_type=MESH
        )

    def arrived(dst, recv):
        remote(dst, dst, ys.at[0], recv, (i, up(1))).wait_recv()

    def sent(src, send):
        remote(src, src, send, yr.at[0, 0], (i, up(1))).wait_send()

    raws = ((gg_ref, lg_ref), (gu_ref, lu_ref), (gd_ref, ld_ref))
    for m in range(3):
        for k in range(2):
            pltpu.make_async_copy(raws[m][k], raw.at[m, k], rawsem.at[m, k]).start()

    barrier = pltpu.get_barrier_semaphore()
    for d in range(1, NY):
        pl.semaphore_signal(barrier, inc=1, device_id=(i, up(d)), device_id_type=MESH)
    for d in (1, -1, 2, -2, 3, -3):
        pl.semaphore_signal(barrier, inc=1, device_id=zdev(d), device_id_type=MESH)
    for d in range(1, 8):
        pl.semaphore_signal(barrier, inc=1, device_id=(8 * z + lax.rem(own + d, 8), y), device_id_type=MESH)

    s_own = z // 2
    order = [up(d) for d in ORDER]

    def block(s, f):
        return blk.at[f, pl.ds(pl.multiple_of(TOK * s, TOK), TOK), :]

    @pl.when(owner)
    def _():
        expert = lax.broadcasted_iota(jnp.int32, (EXPERTS, TOK), 0)
        hit = jnp.zeros((EXPERTS, TOK), F32)
        weight = jnp.zeros((EXPERTS, TOK), F32)
        gains = wt_ref[...].astype(F32)
        for k in range(8):
            same = expert == rt_ref[k : k + 1, :]
            hit = hit + jnp.where(same, 1.0, 0.0)
            weight = weight + jnp.where(same, gains[k : k + 1, :], 0.0)
        before = lax.broadcasted_iota(jnp.int32, (TOK, TOK), 0) < lax.broadcasted_iota(jnp.int32, (TOK, TOK), 1)
        slot = dot_nn(hit.astype(BF16), jnp.where(before, 1.0, 0.0).astype(BF16))
        aux[s_own, 0:EXPERTS, :] = jnp.where(hit > 0.0, slot, -1000.0)
        aux[s_own, EXPERTS:, :] = weight

    pl.semaphore_wait(barrier, 3 + 6 + 7)

    halves = ((tok_ref, slice(0, QD)), (cot_ref, slice(QD, 2 * QD)))

    def token_send(h):
        src, lanes = halves[h]
        return remote(src, block(s_own, y).at[:, lanes], ys.at[h], yr.at[y, h], (i, yb))

    def token_keep(h):
        src, lanes = halves[h]
        return pltpu.make_async_copy(src, block(s_own, y).at[:, lanes], yr.at[y, h])

    for h in range(2):

        @pl.when(jnp.logical_not(owner))
        def _():
            token_send(h).start()

        @pl.when(owner)
        def _():
            token_keep(h).start()

    def piece(s, k):
        if k == PIECES:
            return aux.at[s]
        return block(s, order[k // 2]).at[:, halves[k % 2][1]]

    def zcopy(n, s, k):
        return remote(piece(s, k), piece(s, k), zs.at[int(n < 0), abs(n) - 1, k], zr.at[s, k], zdev(n))

    def zgot(s, k):
        arrived(piece(s, k), zr.at[s, k])

    def give(k):
        zcopy(1, s_own, k).start()
        zcopy(-1, s_own, k).start()

    def with_extra(k):
        return (PIECES, 0) if k == 0 else (k,)

    @pl.when(source)
    def _():
        give(PIECES)
        for h in range(2):
            token_keep(h).wait()
            give(h)

    diagonal = lax.broadcasted_iota(jnp.int32, (HID, HID), 0) == lax.broadcasted_iota(jnp.int32, (HID, HID), 1)

    def column_of(ref):
        return jnp.sum(jnp.where(diagonal, ref[...], 0.0), axis=1, keepdims=True)

    sco[0, 0:HID, :] = column_of(sg_ref)
    sco[1, 0:HID, :] = column_of(su_ref)

    def scale_of(m, at, n):
        return sd_ref[...] if m == 2 else sco[m, pl.ds(at, n), :]

    def wcopy(m):
        return remote(wf.at[m, 0:HID, :], wf.at[m, HID:HH, :], ws.at[m], wr.at[m], (i, wpair))

    def soften(m):
        for k in range(2):
            pltpu.make_async_copy(raws[m][k], raw.at[m, k], rawsem.at[m, k]).wait()

        @pl.loop(0, HID // 16)
        def _(t):
            at = pl.multiple_of(16 * t, 16)
            grid = raw[m, 0, pl.ds(at, 16), :].astype(F32)
            latent = raw[m, 1, pl.ds(at, 16), :].astype(F32)
            level = grid + 0.5 * (1.0 + jnp.tanh(latent / temper))
            wf[m, pl.ds(at, 16), :] = (level * scale_of(m, at, 16)).astype(BF16)

        wcopy(m).start()

    soften(0)
    soften(1)
    soften(2)

    def give_next(k):
        arrived(piece(s_own, k), yr.at[order[k // 2], k % 2])
        give(k)

    @pl.when(source)
    def _():
        for k in range(2, AHEAD + 2):
            give_next(k)

    def relay_piece(k):
        for n, side in ((-1, 1), (1, -1)):
            zgot(zat(n) // 2, k)
            zcopy(side, zat(n) // 2, k).start()
            zcopy(2 * side, zat(n) // 2, k).start()
            if (side == 1) == (k % 2 == 0):
                zcopy(3 * side, zat(n) // 2, k).start()

    @pl.when(relay)
    def _():
        for k in (PIECES, *range(AHEAD)):
            relay_piece(k)

    def rowpart(xsrc, lanes):
        return rows.at[pl.ds(pl.multiple_of(SRC * xsrc, SRC), SRC), lanes]

    def out_lanes(k):
        return slice(0, EXTRA) if k == PIECES else lanes_of(order[k // 2], k % 2)

    def row_send(d, k):
        j = lax.rem(own + d, 8)
        src = sendbuf.at[pl.ds(pl.multiple_of(SRC * j, SRC), SRC), out_lanes(k)]
        if d == 0:
            return pltpu.make_async_copy(src, rowpart(x, out_lanes(k)), xr.at[k, x])
        return remote(src, rowpart(x, out_lanes(k)), xs.at[k, d], xr.at[k, x], (8 * z + j, y))

    def swap_rows(k):
        return remote(
            rows.at[0:ROWS, out_lanes(k)], rows.at[ROWS : 2 * ROWS, out_lanes(k)], fs.at[k], fr.at[k], (i, rpair)
        )

    def forward(k):
        for g in with_extra(k):
            for xsrc in range(NX):
                arrived(rowpart(xsrc, out_lanes(g)), xr.at[g, xsrc])
            swap_rows(g).start()

    for k in range(PIECES):

        @pl.when(source)
        def _():
            for g in with_extra(k):
                for n in (2, -2, 4):
                    zgot(zat(n) // 2, g)

        @pl.when(relay)
        def _():
            for g in with_extra(k):
                for n in (3, -3):
                    zgot(zat(n) // 2, g)

        @pl.when(column)
        def _():
            if k == 0:
                slots = [aux[s, pl.ds(pl.multiple_of(8 * z, 8), 8), :] + float(CAP * s) for s in range(4)]
                gains = [aux[s, pl.ds(pl.multiple_of(EXPERTS + 8 * z, 8), 8), :] for s in range(4)]
                slots, gains = jnp.concatenate(slots, axis=1), jnp.concatenate(gains, axis=1)
                place = lax.broadcasted_iota(jnp.int32, (SRC, 4 * TOK), 0).astype(F32)
                for j in range(8):
                    chosen = place == slots[j : j + 1, :]
                    smat[SRC * j : SRC * (j + 1), :] = jnp.where(chosen, 1.0, 0.0).astype(BF16)
                    gain = jnp.sum(jnp.where(chosen, gains[j : j + 1, :], 0.0), axis=1, keepdims=True)
                    sendbuf[SRC * j : SRC * (j + 1), 0:EXTRA] = jnp.broadcast_to(gain, (SRC, EXTRA)).astype(BF16)
            picked = dot_nn(smat[...], blk[order[k // 2], :, halves[k % 2][1]])
            sendbuf[:, out_lanes(k)] = picked.astype(BF16)
            for g in with_extra(k):
                for d in range(8):
                    row_send(d, g).start()

        @pl.when(source)
        def _():
            if k + AHEAD + 2 < PIECES:
                give_next(k + AHEAD + 2)

        @pl.when(relay)
        def _():
            if k + AHEAD < PIECES:
                relay_piece(k + AHEAD)

        if k >= 1:
            forward(k - 1)
    forward(PIECES - 1)

    @pl.when(column)
    def _():
        for t in range(4):
            lanes = slice(TOK * t, TOK * (t + 1))
            smt[lanes, :] = smat[:, lanes].astype(F32).T.astype(BF16)

    for m in range(3):
        wcopy(m).wait_recv()

    def hidden(r):
        part_rows = slice(ROWS * r, ROWS * (r + 1))
        for out, m, h in ((gs, 0, 0), (us, 1, 0), (bh, 2, 1)):
            total = None
            for f in range(NY):
                term = dot_nt(rows[part_rows, going(f, h)], wf[m, :, feature(f)])
                total = term if total is None else total + term
            out[...] = total

    def gradients(r):
        @pl.loop(0, ROWS // 128)
        def _(t):
            at = pl.multiple_of(128 * t, 128)
            here = pl.ds(at, 128)
            g, u, back = gs[here, :], us[here, :], bh[here, :]
            weight = rows[pl.ds(pl.multiple_of(ROWS * r + at, 128), 128), 0:EXTRA][:, 0:1].astype(F32)
            sigma = jax.nn.sigmoid(g)
            active = g * sigma
            value = active * u
            score = jnp.sum(value * back, axis=1, keepdims=True)
            delta = back * weight
            there = pl.ds(pl.multiple_of(ROWS * r + at, 128), 128)
            d_gate = delta * u * sigma * (1.0 + g * (1.0 - sigma))
            d_up = delta * active
            dg[here, :] = d_gate.astype(BF16)
            du[here, :] = d_up.astype(BF16)
            sco[2 + r, here, :] = score
            lt[0, :, there] = d_gate.T.astype(BF16)
            lt[1, :, there] = d_up.T.astype(BF16)
            lt[2, :, there] = (value * weight).T.astype(BF16)

    def back_of(f):
        return dot_nn(dg[...], wf[0, :, feature(f)]) + dot_nn(du[...], wf[1, :, feature(f)])

    lane = lax.broadcasted_iota(jnp.int32, (ROWS, EXTRA), 1)

    def split(score):
        high = score.astype(BF16).astype(F32)
        spread = jnp.where(lane == i, high, 0.0) + jnp.where(lane == i + EXPERTS, score - high, 0.0)
        return spread.astype(BF16)

    def swap_back(f):
        return remote(bsend.at[:, coming(f)], bgot.at[:, coming(f)], es.at[f], er.at[f], (i, rpair))

    hidden(0)
    gradients(0)
    for f in range(NY):
        bown[:, feature(f)] = back_of(f)
    arrived(rows.at[ROWS : 2 * ROWS, 0:EXTRA], fr.at[PIECES])
    for k in range(PIECES):
        f = lax.rem(rpair + ORDER[k // 2], NY)
        arrived(rows.at[ROWS : 2 * ROWS, lanes_of(f, k % 2)], fr.at[k])
        here = rows[ROWS : 2 * ROWS, lanes_of(f, k % 2)]
        for out, m in ((bh, 2),) if k % 2 else ((gs, 0), (us, 1)):
            term = dot_nt(here, wf[m, :, pl.ds(pl.multiple_of(QD * f, QD), QD)])
            out[...] = term if k < 2 else out[...] + term
    gradients(1)
    for f in range(NY):
        bsend[:, feature(f)] = back_of(f).astype(BF16)
        if f == NY - 1:
            score = sco[3, :, :]
            high = score.astype(BF16).astype(F32)
            spread = jnp.where(lane == 0, high, 0.0) + jnp.where(lane == 1, score - high, 0.0)
            bsend[:, D:] = spread.astype(BF16)
        swap_back(f).start()

    def gcopy(m):
        return remote(grad.at[m, HID:HH, :], rr.at[m], gsend.at[m], grecv.at[m], (i, wpair))

    def outer(m):
        h = 1 if m == 2 else 0
        for f in range(NY):
            grad[m, :, feature(f)] = dot_nn(lt[m], rows[:, going(f, h)]).astype(BF16)

    def back_send(d, f):
        xsrc = lax.rem(x + d, NX)
        return remote(
            br.at[pl.ds(pl.multiple_of(SRC * xsrc, SRC), SRC), coming(f)],
            rb.at[pl.ds(pl.multiple_of(SRC * own, SRC), SRC), coming(f)],
            bs.at[f, d], brr.at[f, own], (8 * z + 2 * xsrc + y // 2, y),
        )

    def give_back(f):
        swap_back(f).wait_recv()
        br[:, feature(f)] = (bown[:, feature(f)] + bgot[:, feature(f)].astype(F32)).astype(BF16)
        if f == NY - 1:
            other = bgot[:, D:].astype(F32)
            br[:, D:] = split(sco[2, :, :] + (other[:, 0:1] + other[:, 1:2]))
        for d in range(1, NX):
            back_send(d, f).start()

        @pl.when(column)
        def _():
            pltpu.make_async_copy(
                br.at[pl.ds(pl.multiple_of(SRC * x, SRC), SRC), coming(f)],
                rb.at[pl.ds(pl.multiple_of(SRC * own, SRC), SRC), coming(f)], brr.at[f, own],
            ).start()

        @pl.when(jnp.logical_not(column))
        def _():
            back_send(0, f).start()

    def plane(s, f):
        return part.at[pl.ds(pl.multiple_of(TOK * s, TOK), TOK), coming(f)]

    def zback(src, n, slot, f):
        return remote(src, zb.at[slot, :, coming(f)], zbs.at[f, slot], zbr.at[f, slot], zdev(n))

    def got(slot, f):
        arrived(zb.at[slot, :, coming(f)], zbr.at[f, slot])
        return zb[slot, :, coming(f)].astype(F32)

    def mine(n, f):
        return plane(zat(n) // 2, f)

    def combine(f):
        for j in range(8):
            arrived(rb.at[pl.ds(SRC * j, SRC), coming(f)], brr.at[f, j])
        part[:, coming(f)] = dot_nn(smt[...], rb[:, coming(f)]).astype(BF16)

    def last(f):
        @pl.when(y == f)
        def _():
            pltpu.make_async_copy(fb.at[:, feature(f)], tg, lr.at[0]).start()

        @pl.when(y != f)
        def _():
            remote(fb.at[:, feature(f)], tg, ls.at[f], lr.at[0], (i, f)).start()

    def last_score(d):
        src = fb.at[:, D:]
        if d == 0:
            return pltpu.make_async_copy(src, sc, lr.at[1])
        return remote(src, sc, ls.at[NY + d], lr.at[1], (i, up(d)))

    def one(f):
        @pl.when(column)
        def _():
            combine(f)

        @pl.when(source)
        def _():
            zback(mine(-2, f), -1, 0, f).start()
            zback(mine(2, f), 1, 1, f).start()
            zback(mine(4, f), -3 if f < 2 else 3, 4, f).start()

        @pl.when(relay)
        def _():
            zback(mine(-3, f), -2, 2, f).start()
            zback(mine(3, f), 2, 3, f).start()

    def two(f):
        @pl.when(relay)
        def _():
            for side, n in ((0, -1), (1, 1)):
                total = mine(n, f)[...].astype(F32) + (got(side, f) + got(2 + side, f))
                if (f < 2) == (side == 0):
                    total = total + got(4, f)
                zt[side, :, coming(f)] = total.astype(BF16)
                zback(zt.at[side, :, coming(f)], n, side, f).start()

    def three(f):
        @pl.when(source)
        def _():
            fb[:, coming(f)] = (mine(0, f)[...].astype(F32) + (got(0, f) + got(1, f))).astype(BF16)
            last(f)
            if f == NY - 1:
                for d in range(NY):
                    last_score(d).start()

    outer(2)
    give_back(0)
    outer(0)
    give_back(1)
    one(0)
    outer(1)
    give_back(2)
    one(1)
    two(0)
    give_back(3)
    for m in (2, 0, 1):
        gcopy(m).start()
    one(2)
    two(1)
    three(0)
    one(3)
    two(2)
    three(1)
    two(3)
    three(2)
    three(3)

    def finish(m, out):
        gcopy(m).wait_recv()

        @pl.loop(0, HID // 16)
        def _(t):
            at = pl.multiple_of(16 * t, 16)
            here = pl.ds(at, 16)
            slope = jnp.tanh(raw[m, 1, here, :].astype(F32) / temper)
            total = grad[m, here, :].astype(F32) + rr[m, here, :].astype(F32)
            value = grad_factor * total * scale_of(m, at, 16) * (1.0 - slope * slope) / (2.0 * temper)
            out[here, :] = value.astype(BF16)

    finish(2, od_ref)
    finish(0, og_ref)
    finish(1, ou_ref)

    arrived(tg, lr.at[0])
    arrived(sc, lr.at[1])
    tgrad_ref[...] = tg[...]
    turned = sc[...].astype(F32).T
    known = turned[0:EXPERTS, :] + turned[EXPERTS:, :]
    expert = lax.broadcasted_iota(jnp.int32, (EXPERTS, TOK), 0)
    for k in range(8):
        same = expert == rt_ref[k : k + 1, :]
        rgrad_ref[k : k + 1, :] = jnp.sum(jnp.where(same, known, 0.0), axis=0, keepdims=True)

    @pl.when(jnp.logical_not(owner))
    def _():
        for h in range(2):
            token_send(h).wait_send()

    @pl.when(owner)
    def _():
        for d in range(1, NY):
            last_score(d).wait_send()
        for f in range(NY):

            @pl.when(y != f)
            def _():
                sent(tg, ls.at[f])

    for m in range(3):
        wcopy(m).wait_send()
        gcopy(m).wait_send()
    for k in range(PIECES + 1):
        swap_rows(k).wait_send()

        @pl.when(column)
        def _():
            for d in range(1, 8):
                row_send(d, k).wait_send()

    for f in range(NY):
        swap_back(f).wait_send()
        for d in range(1, NX):
            back_send(d, f).wait_send()

        @pl.when(jnp.logical_not(column))
        def _():
            back_send(0, f).wait_send()

        @pl.when(column)
        def _():
            for slot in range(2):
                zback(mine(0, f), 1, slot, f).wait_send()

        @pl.when(source)
        def _():
            zback(mine(0, f), 1, 4, f).wait_send()

        @pl.when(relay)
        def _():
            for slot in range(2, 4):
                zback(mine(0, f), 1, slot, f).wait_send()

    for k in range(PIECES + 1):

        @pl.when(source)
        def _():
            for n in (1, -1):
                zcopy(n, s_own, k).wait_send()

        @pl.when(relay)
        def _():
            for n in (1, -1, 2, -2, 3 if k % 2 == 0 else -3):
                zcopy(n, s_own, k).wait_send()


def exchange(*operands):
    vmem = pl.BlockSpec(memory_space=pltpu.VMEM)
    whole = pl.BlockSpec(memory_space=pl.ANY)
    dma = pltpu.SemaphoreType.DMA
    return pl.pallas_call(
        kernel,
        out_shape=(
            jax.ShapeDtypeStruct((HID, D), BF16),
            jax.ShapeDtypeStruct((HID, D), BF16),
            jax.ShapeDtypeStruct((HID, D), BF16),
            jax.ShapeDtypeStruct((TOK, QD), BF16),
            jax.ShapeDtypeStruct((8, TOK), F32),
        ),
        in_specs=[whole] * 2 + [vmem] * 2 + [whole] * 6 + [vmem] * 3,
        out_specs=(vmem,) * 5,
        scratch_shapes=[
            pltpu.VMEM((3, 2, HID, D), BF16),
            pltpu.VMEM((3, HH, D), BF16),
            pltpu.VMEM((3, HH, D), BF16),
            pltpu.VMEM((3, HID, D), BF16),
            pltpu.VMEM((NY, 4 * TOK, 2 * QD), BF16),
            pltpu.VMEM((4, 2 * EXPERTS, TOK), F32),
            pltpu.VMEM((8 * SRC, 2 * D + EXTRA), BF16),
            pltpu.VMEM((2 * ROWS, 2 * D + EXTRA), BF16),
            pltpu.VMEM((8 * SRC, 4 * TOK), BF16),
            pltpu.VMEM((4 * TOK, 8 * SRC), BF16),
            pltpu.VMEM((ROWS, HH), F32),
            pltpu.VMEM((ROWS, HH), F32),
            pltpu.VMEM((ROWS, HH), F32),
            pltpu.VMEM((4, ROWS, 1), F32),
            pltpu.VMEM((ROWS, HH), BF16),
            pltpu.VMEM((ROWS, HH), BF16),
            pltpu.VMEM((3, HH, 2 * ROWS), BF16),
            pltpu.VMEM((ROWS, D), F32),
            pltpu.VMEM((ROWS, D + EXTRA), BF16),
            pltpu.VMEM((ROWS, D + EXTRA), BF16),
            pltpu.VMEM((ROWS, D + EXTRA), BF16),
            pltpu.VMEM((8 * SRC, D + EXTRA), BF16),
            pltpu.VMEM((4 * TOK, D + EXTRA), BF16),
            pltpu.VMEM((5, TOK, D + EXTRA), BF16),
            pltpu.VMEM((2, TOK, D + EXTRA), BF16),
            pltpu.VMEM((TOK, D + EXTRA), BF16),
            pltpu.VMEM((TOK, QD), BF16),
            pltpu.VMEM((TOK, EXTRA), BF16),
            dma((3, 2)),
            dma((3,)),
            dma((3,)),
            dma((3,)),
            dma((3,)),
            dma((2,)),
            dma((NY, 2)),
            dma((2, 3, PIECES + 1)),
            dma((4, PIECES + 1)),
            dma((PIECES + 1, 8)),
            dma((PIECES + 1, NX)),
            dma((PIECES + 1,)),
            dma((PIECES + 1,)),
            dma((NY,)),
            dma((NY,)),
            dma((NY, NX)),
            dma((NY, 8)),
            dma((NY, 5)),
            dma((NY, 5)),
            dma((2 * NY,)),
            dma((2,)),
        ],
        compiler_params=pltpu.CompilerParams(
            collective_id=0, has_side_effects=True, vmem_limit_bytes=64 * 1024 * 1024 - 256 * 1024
        ),
    )(*operands)


def body(
    tokens, cotangent, route_weights, routes,
    grid_gate, latent_gate, scale_gate,
    grid_up, latent_up, scale_up,
    grid_down, latent_down, scale_down,
):
    grad_gate, grad_up, grad_down, token_grad, route_grad = exchange(
        tokens, cotangent, routes.T, route_weights.T,
        grid_gate[0], latent_gate[0], grid_up[0], latent_up[0], grid_down[0], latent_down[0],
        scale_gate, scale_up, scale_down,
    )
    return (
        grad_gate.astype(F32)[None], grad_up.astype(F32)[None], grad_down.astype(F32)[None],
        token_grad, route_grad.T,
    )


def solution(mesh):
    return jax.shard_map(
        body,
        mesh=mesh,
        in_specs=(
            P("ep", "tp"), P("ep", "tp"), P("ep", None), P("ep", None),
            P("ep", "tp", None), P("ep", "tp", None), P("ep", "tp"),
            P("ep", "tp", None), P("ep", "tp", None), P("ep", "tp"),
            P("ep", "tp", None), P("ep", "tp", None), P("ep", None),
        ),
        out_specs=(
            P("ep", "tp", None), P("ep", "tp", None), P("ep", "tp", None), P("ep", "tp"), P("ep", None),
        ),
        check_vma=False,
    )
```
